32 devices in a mesh: rad: 4 (over y, x), lat: 8 (over z, core).
Axes of the slice: x: 2, y: 2, z: 4, core: 2. Of those that a mesh axis runs over, the one named last changes fastest.
Arguments:
- entropy: bfloat16 [256, 768, 1536], P('rad', 'lat'), may hold values from -6 to 6
- radial_flow: bfloat16 [256, 768, 1536], P('rad', 'lat'), may hold values from -6 to 6
- slope: float32 [256], P('rad'), may hold values from 0.5 to 2
- gravity: float32 [256], P('rad'), may hold values from 0.5 to 2
- pair_slot: int32 [256], P('lat'), may hold values from 0 to 255, each once
- analysis: bfloat16 [256, 768, 513], P('lat', 'rad'), may hold values from -0.21875 to 0.21875
- rad_right: bfloat16 [2, 256, 256], replicated, may hold values from -0.375 to 0.375
- rad_left: bfloat16 [2, 256, 256], replicated, may hold values from -0.375 to 0.375
- rad_rates: float32 [2, 256], replicated, may hold values from 0.25 to 2
Outputs:
- solved: bfloat16 [256, 2, 256, 2, 513], P('lat', None, 'rad')
The draws below stay inside these ranges and needn't reach their ends.
Inputs may be any that keep to these rules, and one draw needn't show every extreme that they name: pair_slot is a permutation: slot s holds the orders pair_slot[s] and 511 - pair_slot[s], and every pair is in exactly one slot.
All inputs are finite; a program needn't handle non-finite values.
Results may differ from the reference program's by a relative error of at most 0.0072.
Values may be sent and summed in bfloat16 or wider, within the bound.
No kernel may reach another device: no remote copies, remote signals or barrier semaphores. Data moves between devices by JAX's collectives and lax.ppermute only.
A program may use at most 256 MiB of HBM per device.

```python
import math
import jax
import jax.numpy as jnp
from jax import lax

NL = 512
NTH = 768
NPHI = 1536
NR = 256
NPAIR = 256
NK = 513


def block_levels(stream_key, shape, split, least, high):
    loudness = 1.0
    for dim, blocks in split:
        draws = jax.random.uniform(jax.random.fold_in(jax.random.fold_in(stream_key, 6), dim), (blocks,), jnp.float32, least / len(split), high / len(split))
        loudness = loudness * jnp.repeat(jnp.exp(draws), shape[dim] // blocks).reshape((-1,) + (1,) * (len(shape) - 1 - dim))
    return loudness


def normal_values(own_key, shape, deviation, limit, shards=(), kind=jnp.bfloat16):
    drawn = deviation * jax.random.normal(own_key, shape, jnp.float32)
    if shards:
        drawn = drawn * block_levels(own_key, shape, shards, -0.22, 0.18)
    return jnp.clip(drawn, -limit, limit).astype(kind)


def setup_inputs(seed: int = 0) -> dict:
    streams_of = jax.random.split(jax.random.key(seed), 10)
    return {
        "entropy": normal_values(streams_of[0], (NR, NTH, NPHI), 1.0, 6.0, ((0, 4), (1, 8))),
        "radial_flow": normal_values(streams_of[1], (NR, NTH, NPHI), 1.0, 6.0, ((0, 4), (1, 8))),
        "slope": jnp.clip(jnp.exp(math.log(2.0) - 1.3862944 * jax.random.uniform(streams_of[2], (NR,), jnp.float32) ** block_levels(streams_of[2], (NR,), ((0, 4),), -0.2, 0.2)), 0.5, 2.0),
        "gravity": jnp.clip(jnp.exp(math.log(2.0) - 1.3862944 * jax.random.uniform(streams_of[3], (NR,), jnp.float32) ** block_levels(streams_of[3], (NR,), ((0, 4),), -0.2, 0.2)), 0.5, 2.0),
        "pair_slot": jax.random.permutation(streams_of[4], NPAIR).astype(jnp.int32),
        "analysis": normal_values(streams_of[5], (NPAIR, NTH, NK), NTH ** -0.5, 0.21875, ((0, 8), (1, 4))),
        "rad_right": normal_values(streams_of[6], (2, NR, NR), NR ** -0.5, 0.375),
        "rad_left": normal_values(streams_of[7], (2, NR, NR), NR ** -0.5, 0.375),
        "rad_rates": jnp.clip(jnp.exp(jax.random.uniform(streams_of[8], (2, NR), jnp.float32, math.log(0.25), math.log(2.0))), 0.25, 2.0),
    }


def transform_table(orders):
    phase_index = jnp.arange(NPHI, dtype=jnp.int32)
    turn_count = phase_index[:, None] * orders[None, :] % NPHI
    angles = turn_count.astype(jnp.float32) * (2.0 * math.pi / NPHI)
    scaling = 1.0 / math.sqrt(NPHI)
    return jnp.concatenate([jnp.cos(angles) * scaling, -jnp.sin(angles) * scaling], axis=1).astype(jnp.bfloat16)

def reference(entropy, radial_flow, slope, gravity, pair_slot, analysis, rad_right, rad_left, rad_rates):
    basis_table = transform_table(jnp.arange(NL, dtype=jnp.int32))

    def one_radius(inputs):
        entropy_f = inputs[0].astype(jnp.float32)
        flow_f = inputs[1].astype(jnp.float32)
        heating = -flow_f * (inputs[2] + entropy_f)
        buoyant = inputs[3] * entropy_f - 0.5 * flow_f * flow_f
        sources = jnp.stack([heating, buoyant]).astype(jnp.bfloat16)
        spectrum = jnp.dot(sources.reshape(2 * NTH, NPHI), basis_table, preferred_element_type=jnp.float32)
        return spectrum.astype(jnp.bfloat16).reshape(2, NTH, 2 * NL)
    spectra = lax.map(one_radius, (entropy, radial_flow, slope, gravity))
    column_index = jnp.arange(NK, dtype=jnp.int32)

    def one_slot(inputs):
        pair_id = inputs[0]
        slot_table = inputs[1]
        columns = jnp.stack([pair_id, NL + pair_id, NL - 1 - pair_id, 2 * NL - 1 - pair_id]).astype(jnp.int32)
        gathered = jnp.take(spectra, columns, axis=3)
        raw_sums = jnp.einsum('rftq,tk->qfrk', gathered.astype(jnp.float32), slot_table.astype(jnp.float32))
        first_part = column_index < NL - pair_id
        coefficient = jnp.where(first_part, raw_sums[:2], raw_sums[2:]).astype(jnp.bfloat16)
        degree = jnp.where(first_part, pair_id + column_index, column_index - 1).astype(jnp.float32)
        damping = 1.0 / (rad_rates[:, :, None] + 2.0 * degree * (degree + 1.0) / (NL * NL))
        mixed_sum = jnp.einsum('cfrk,fqr->cfqk', coefficient.astype(jnp.float32), rad_right.astype(jnp.float32))
        scaled = (mixed_sum * damping[None]).astype(jnp.bfloat16)
        result = jnp.einsum('cfqk,frq->frck', scaled.astype(jnp.float32), rad_left.astype(jnp.float32))
        return result.astype(jnp.bfloat16)
    return lax.map(one_slot, (pair_slot, analysis))
```

```python
import functools
import math

import jax
import jax.numpy as jnp
from jax import lax
from jax.experimental import pallas as pl
from jax.experimental.pallas import tpu as pltpu
from jax.sharding import PartitionSpec as P

LANES = 128
STEP = 16
VMEM_BYTES = 56 * 1024 * 1024


def transform_block(rows_ref, basis_ref, out_ref, product_s, out_s):
    fields, radii, step, longitudes = rows_ref.shape
    dests, columns = out_ref.shape[0], out_ref.shape[1]
    blocks = dests * columns // LANES
    for f in range(fields):
        product = jnp.dot(
            rows_ref[f].reshape(radii * step, longitudes),
            basis_ref[...],
            preferred_element_type=jnp.float32,
        )
        for b in range(blocks):
            product_s[b, f * radii * step : (f + 1) * radii * step, :] = product[
                :, b * LANES : (b + 1) * LANES
            ]
    for t in range(step):
        for b in range(blocks):
            turned = product_s[b, pl.ds(t, fields * radii, stride=step), :].T
            out_s[pl.ds(b * LANES * step + t, LANES, stride=step), :] = turned
    out_ref[...] = out_s[...].reshape(dests, columns, step, fields * radii).astype(jnp.bfloat16)


def first_fourier_kernel(
    slope, gravity, entropy_ref, flow_ref, basis_ref, out_ref, rows_ref, product_s, out_s
):
    radii = entropy_ref.shape[0]

    def radius(r, carry):
        entropy_f = entropy_ref[r].astype(jnp.float32)
        flow_f = flow_ref[r].astype(jnp.float32)
        heating = -flow_f * (slope[r] + entropy_f)
        buoyant = gravity[r] * entropy_f - 0.5 * flow_f * flow_f
        rows_ref[0, r] = heating.astype(jnp.bfloat16)
        rows_ref[1, r] = buoyant.astype(jnp.bfloat16)
        return carry

    lax.fori_loop(0, radii, radius, 0)
    transform_block(rows_ref, basis_ref, out_ref, product_s, out_s)


def fourier_specs(fields, radii, longitudes, basis, dests):
    columns = basis.shape[1] // dests
    width = fields * radii
    rows = pl.BlockSpec((fields, radii, STEP, longitudes), lambda i, *_: (0, 0, i, 0))
    table = pl.BlockSpec(basis.shape, lambda i, *_: (0, 0), pipeline_mode=pl.Buffered(1))
    out = pl.BlockSpec((dests, columns, STEP, width), lambda i, *_: (0, 0, i, 0))
    scratch = [
        pltpu.VMEM((dests * columns // LANES, width * STEP, LANES), jnp.float32),
        pltpu.VMEM((dests * columns * STEP, width), jnp.float32),
    ]
    return columns, rows, table, out, scratch


def first_fourier(entropy, flow, slope, gravity, basis, dests):
    radii, colats, longitudes = entropy.shape
    columns, rows, table, out, scratch = fourier_specs(2, radii, longitudes, basis, dests)
    grid_in = pl.BlockSpec((radii, STEP, longitudes), lambda i, *_: (0, i, 0))
    return pl.pallas_call(
        first_fourier_kernel,
        grid_spec=pltpu.PrefetchScalarGridSpec(
            num_scalar_prefetch=2,
            grid=(colats // STEP,),
            in_specs=[grid_in, grid_in, table],
            out_specs=[out, rows],
            scratch_shapes=scratch,
        ),
        out_shape=[
            jax.ShapeDtypeStruct((dests, columns, colats, 2 * radii), jnp.bfloat16),
            jax.ShapeDtypeStruct((2,) + entropy.shape, jnp.bfloat16),
        ],
        compiler_params=pltpu.CompilerParams(vmem_limit_bytes=VMEM_BYTES),
        cost_estimate=pl.CostEstimate(
            flops=4 * entropy.size * basis.shape[1],
            bytes_accessed=8 * entropy.size,
            transcendentals=0,
        ),
        name="first_fourier",
    )(slope, gravity, entropy, flow, basis)


def next_fourier(rows_in, basis, dests):
    fields, radii, colats, longitudes = rows_in.shape
    columns, rows, table, out, scratch = fourier_specs(fields, radii, longitudes, basis, dests)
    return pl.pallas_call(
        transform_block,
        grid=(colats // STEP,),
        in_specs=[rows, table],
        out_specs=out,
        out_shape=jax.ShapeDtypeStruct((dests, columns, colats, fields * radii), jnp.bfloat16),
        scratch_shapes=scratch,
        compiler_params=pltpu.CompilerParams(vmem_limit_bytes=VMEM_BYTES),
        cost_estimate=pl.CostEstimate(
            flops=2 * rows_in.size * basis.shape[1],
            bytes_accessed=2 * rows_in.size,
            transcendentals=0,
        ),
        name="next_fourier",
    )(rows_in, basis)


def legendre_kernel(rads, scalars, spectra_ref, table_ref, *out_refs):
    sources, _, _, colats, width = spectra_ref.shape
    parts, _, part, count = table_ref.shape
    per_rad = pl.num_programs(1)
    m, i = pl.program_id(0), pl.program_id(1)
    me = scalars[0]
    pair = scalars[1 + (me ^ m) * per_rad + i]
    columns = jnp.concatenate(
        [spectra_ref[:, 0, q].reshape(sources * colats, width) for q in range(4)], axis=1
    )
    raw = lax.dot_general(
        columns,
        table_ref[:, 0].reshape(parts * part, count),
        (((0,), (0,)), ((), ())),
        preferred_element_type=jnp.float32,
    )
    k = lax.broadcasted_iota(jnp.int32, (width, count), 1)
    first = k < count - 1 - pair
    radii = width // 2
    for c in range(2):
        value = jnp.where(
            first, raw[c * width : (c + 1) * width], raw[(2 + c) * width : (3 + c) * width]
        ).astype(jnp.bfloat16)
        for target in range(rads):

            @pl.when(m == target)
            def _():
                for f in range(2):
                    out_refs[target][0, f, c, :, count - 1 :] = jnp.zeros(
                        (radii, out_refs[target].shape[4] - count + 1), jnp.bfloat16
                    )
                    out_refs[target][0, f, c, :, :count] = value[f * radii : (f + 1) * radii]


def legendre(spectra, table, scalars, rads, base):
    sources, slots, _, colats, width = spectra.shape
    parts, _, part, count = table.shape
    per_rad = slots // rads

    def slot_of(m, i, s):
        return (s[0] ^ m) * per_rad + i

    def out_map(target):
        def index(m, i, s):
            return (jnp.clip(m * per_rad + i - target * per_rad, 0, per_rad - 1), 0, 0, 0, 0)

        return index

    block = (1, 2, 2, width // 2, pl.cdiv(count, LANES) * LANES)
    return pl.pallas_call(
        functools.partial(legendre_kernel, rads),
        grid_spec=pltpu.PrefetchScalarGridSpec(
            num_scalar_prefetch=1,
            grid=(rads, per_rad),
            in_specs=[
                pl.BlockSpec(
                    (sources, 1, 4, colats, width), lambda m, i, s: (0, slot_of(m, i, s), 0, 0, 0)
                ),
                pl.BlockSpec(
                    (parts, 1, part, count), lambda m, i, s: (0, base + slot_of(m, i, s), 0, 0)
                ),
            ],
            out_specs=[pl.BlockSpec(block, out_map(target)) for target in range(rads)],
        ),
        out_shape=[jax.ShapeDtypeStruct((per_rad,) + block[1:], jnp.bfloat16)] * rads,
        compiler_params=pltpu.CompilerParams(vmem_limit_bytes=VMEM_BYTES),
        cost_estimate=pl.CostEstimate(
            flops=2 * slots * 4 * width * sources * colats * count,
            bytes_accessed=2 * (spectra.size + slots * parts * part * count),
            transcendentals=0,
        ),
        name="legendre",
    )(scalars, spectra, table)


def radial_kernel(rads, degrees, scalars, *refs):
    in_refs, (right_ref, left_ref, rates_ref) = refs[:rads], refs[rads : rads + 3]
    out_refs = refs[rads + 3 : 2 * rads + 3]
    gathered, scaled = refs[2 * rads + 3 :]
    _, _, _, radii, count = in_refs[0].shape
    per_rad = pl.num_programs(0)
    me = scalars[0]
    pair = scalars[1 + me * per_rad + pl.program_id(0)]
    total = rads * radii
    k = lax.broadcasted_iota(jnp.int32, (1, count), 1)
    degree = jnp.where(k < degrees - pair, pair + k, k - 1).astype(jnp.float32)
    decay = 2.0 * degree * (degree + 1.0) / (degrees * degrees)
    damping = 1.0 / (rates_ref[0] + decay)
    for m in range(rads):
        start = pl.multiple_of((me ^ m) * radii, radii)
        for c in range(2):
            gathered[c, pl.ds(start, radii), :] = in_refs[m][0, 0, c]
    for c in range(2):
        mixed = jnp.dot(right_ref[0], gathered[c], preferred_element_type=jnp.float32)
        scaled[c * total : (c + 1) * total] = (mixed * damping).astype(jnp.bfloat16)
    for m in range(rads):
        start = pl.multiple_of((me ^ m) * 2 * radii, 2 * radii)
        out_refs[m][0, 0] = jnp.dot(
            left_ref[0, pl.ds(start, 2 * radii), :], scaled[...], preferred_element_type=jnp.float32
        ).astype(jnp.bfloat16)


def radial(pieces, right, left, rates, scalars, degrees):
    rads = len(pieces)
    per_rad, fields, parts, radii, count = pieces[0].shape
    total = rads * radii
    by_field = lambda shape: pl.BlockSpec((1,) + shape, lambda i, f, s: (f, 0, 0))
    return pl.pallas_call(
        functools.partial(radial_kernel, rads, degrees),
        grid_spec=pltpu.PrefetchScalarGridSpec(
            num_scalar_prefetch=1,
            grid=(per_rad, fields),
            in_specs=[
                pl.BlockSpec((1, 1, parts, radii, count), lambda i, f, s: (i, f, 0, 0, 0))
            ]
            * rads
            + [by_field((total, total)), by_field((2 * total, 2 * total)), by_field((total, 1))],
            out_specs=[pl.BlockSpec((1, 1, 2 * radii, count), lambda i, f, s: (i, f, 0, 0))] * rads,
            scratch_shapes=[
                pltpu.VMEM((2, total, count), jnp.bfloat16),
                pltpu.VMEM((2 * total, count), jnp.bfloat16),
            ],
        ),
        out_shape=[jax.ShapeDtypeStruct((per_rad, fields, 2 * radii, count), jnp.bfloat16)] * rads,
        compiler_params=pltpu.CompilerParams(vmem_limit_bytes=VMEM_BYTES),
        cost_estimate=pl.CostEstimate(
            flops=2 * per_rad * fields * count * total * total * 6,
            bytes_accessed=16 * per_rad * fields * total * count,
            transcendentals=0,
        ),
        name="radial",
    )(scalars, *pieces, right, left, rates)


def place_kernel(rads, scalars, *refs):
    in_refs, out_ref = refs[:rads], refs[-1]
    _, _, radii, _, count = out_ref.shape
    for m in range(rads):

        @pl.when(pl.program_id(0) == m)
        def _():
            for r in range(radii):
                out_ref[0, 0, r] = in_refs[m][0, 0, 2 * r : 2 * r + 2, :count]


def place(pieces, scalars, so_far, slots, base, count):
    rads = len(pieces)
    per_rad, fields, rows, padded = pieces[0].shape

    def in_map(source):
        def index(m, i, f, s):
            step = (m * per_rad + i) * fields + f - source * per_rad * fields
            step = jnp.clip(step, 0, per_rad * fields - 1)
            return (step // fields, step % fields, 0, 0)

        return index

    return pl.pallas_call(
        functools.partial(place_kernel, rads),
        grid_spec=pltpu.PrefetchScalarGridSpec(
            num_scalar_prefetch=1,
            grid=(rads, per_rad, fields),
            in_specs=[pl.BlockSpec((1, 1, rows, padded), in_map(source)) for source in range(rads)]
            + ([] if so_far is None else [pl.BlockSpec(memory_space=pl.ANY)]),
            out_specs=pl.BlockSpec(
                (1, 1, rows // 2, 2, count),
                lambda m, i, f, s: (base + (s[0] ^ m) * per_rad + i, f, 0, 0, 0),
            ),
        ),
        out_shape=jax.ShapeDtypeStruct((slots, fields, rows // 2, 2, count), jnp.bfloat16),
        input_output_aliases={} if so_far is None else {1 + rads: 0},
        compiler_params=pltpu.CompilerParams(vmem_limit_bytes=VMEM_BYTES),
        cost_estimate=pl.CostEstimate(
            flops=0, bytes_accessed=4 * rads * per_rad * fields * rows * count, transcendentals=0
        ),
        name="place",
    )(scalars, *pieces, *([] if so_far is None else [so_far]))


def basis_of(pairs, degrees, longitudes):
    orders = jnp.stack([pairs, degrees - 1 - pairs], axis=2).reshape(-1)
    orders = jnp.repeat(orders, 2)[None, :]
    quarter = (jnp.arange(orders.shape[1], dtype=jnp.int32) % 2 * (longitudes // 4))[None, :]
    turn_count = (jnp.arange(longitudes, dtype=jnp.int32)[:, None] * orders + quarter) % longitudes
    angles = turn_count.astype(jnp.float32) * (2.0 * math.pi / longitudes)
    return (jnp.cos(angles) * (1.0 / math.sqrt(longitudes))).astype(jnp.bfloat16)


def local_chunks(
    sizes,
    entropy, radial_flow, slope, gravity, pair_slot, analysis, rad_right, rad_left, rad_rates,
):
    lats = lax.axis_size("lat")
    rads = lax.axis_size("rad")
    radii, colats, longitudes = entropy.shape
    slots, _, count = analysis.shape
    degrees = count - 1
    width = 2 * radii
    starts = [sum(sizes[:j]) for j in range(len(sizes))]
    me = lax.axis_index("rad").astype(jnp.int32)
    every_pair = lax.all_gather(pair_slot, "lat", axis=0)
    tables = [
        lax.all_gather(analysis[: sizes[0]], "rad", axis=0),
        lax.all_gather(analysis[sizes[0] :], "rad", axis=0),
    ]
    total = rads * radii
    rates = rad_rates[:, :, None]

    def exchange(pieces):
        return [
            piece
            if m == 0
            else lax.ppermute(piece, "rad", [(i, i ^ m) for i in range(rads)])
            for m, piece in enumerate(pieces)
        ]

    def basis_at(pairs, j):
        return basis_of(pairs[:, starts[j] : starts[j] + sizes[j]], degrees, longitudes)

    def after(value, *earlier):
        return lax.optimization_barrier((value,) + earlier)[0]

    def send(spectra):
        return lax.all_to_all(spectra, "lat", 0, 0, tiled=True)

    last = len(sizes) - 1
    scalars = [
        jnp.concatenate([me[None], pair_slot[start : start + size]])
        for start, size in zip(starts, sizes)
    ]
    spectra, rows = first_fourier(
        entropy, radial_flow, slope, gravity, basis_at(every_pair, 0), lats
    )
    arrived = [send(spectra)]
    later_pairs = after(every_pair, rows)
    rad_left = after(rad_left, rows)
    spread = jnp.zeros((2, total, 2, 2, total), jnp.bfloat16)
    spread = spread.at[:, :, 0, 0].set(rad_left).at[:, :, 1, 1].set(rad_left)
    spread = spread.reshape(2, 2 * total, 2 * total)

    def fourier(j, *earlier):
        basis = after(basis_at(later_pairs, j), *earlier)
        return next_fourier(rows, basis, lats)

    def coefs(j, *earlier):
        block = after(arrived[j], *earlier).reshape(lats, sizes[j], 4, colats, width)
        base = 0 if j == 0 else starts[j] - sizes[0]
        return legendre(block, tables[min(j, 1)], scalars[j], rads, base)

    def solve(pieces, j, *earlier):
        pieces = [after(pieces[0], *earlier)] + exchange(pieces)[1:]
        return radial(pieces, rad_right, spread, rates, scalars[j], degrees)

    def put(pieces, j, so_far, *earlier):
        pieces = [after(pieces[0], *earlier)] + exchange(pieces)[1:]
        return place(pieces, scalars[j], so_far, slots, starts[j], count)

    arrived.append(send(fourier(1, tables[0])))
    result, waiting = None, None
    for j in range(last + 1):
        earlier = [] if result is None else [result]
        ahead = None
        if j + 2 <= last:
            ahead = fourier(j + 2, arrived[j], *([] if j == 0 else [tables[1]]), *earlier)
            earlier = [ahead]
        if waiting is not None:
            earlier.append(waiting[0])
        pieces = coefs(j, *earlier)
        if waiting is not None:
            result = put(waiting, j - 1, result, pieces[0])
            waiting = None
            pieces = solve(pieces, j, result)
        else:
            pieces = solve(pieces, j)
        if j == last - 1:
            waiting = pieces
        else:
            result = put(pieces, j, result)
        if ahead is not None:
            arrived.append(send(after(ahead, result)))
    return result


def local_plain(
    entropy, radial_flow, slope, gravity, pair_slot, analysis, rad_right, rad_left, rad_rates
):
    lat_count = lax.axis_size("lat")
    rad_count = lax.axis_size("rad")
    radii, colats, longitudes = entropy.shape
    pair_local = pair_slot.shape[0]
    coef_count = analysis.shape[2]
    degrees = coef_count - 1
    group_total = 2 * pair_local
    group_local = group_total // rad_count
    every_pair = lax.all_gather(pair_slot, "lat", axis=0, tiled=True)
    entropy_f = entropy.astype(jnp.float32)
    flow_f = radial_flow.astype(jnp.float32)
    heating = -flow_f * (slope[:, None, None] + entropy_f)
    buoyant = gravity[:, None, None] * entropy_f - 0.5 * flow_f * flow_f
    sources = jnp.stack([heating, buoyant]).astype(jnp.bfloat16)
    pair_grid = every_pair.reshape(lat_count, 1, pair_local)
    orders = jnp.concatenate([pair_grid, degrees - 1 - pair_grid], axis=1)
    phase_index = jnp.arange(longitudes, dtype=jnp.int32)
    turn_count = phase_index[:, None, None, None] * orders[None] % longitudes
    angles = turn_count.astype(jnp.float32) * (2.0 * math.pi / longitudes)
    scaling = 1.0 / math.sqrt(longitudes)
    basis_table = jnp.stack([jnp.cos(angles) * scaling, -jnp.sin(angles) * scaling], axis=3)
    basis_table = basis_table.reshape(longitudes, lat_count * 4 * pair_local).astype(jnp.bfloat16)
    spectra = jnp.einsum(
        "frtj,jc->cfrt", sources, basis_table, preferred_element_type=jnp.float32
    ).astype(jnp.bfloat16)
    column_index = jnp.arange(coef_count, dtype=jnp.int32)
    group_index = lax.axis_index("rad") * group_local + jnp.arange(group_local, dtype=jnp.int32)
    group_slot = group_index // 2
    group_field = group_index % 2
    slot_match = jnp.arange(pair_local, dtype=jnp.int32)[None, :] == group_slot[:, None]
    group_pair = jnp.sum(jnp.where(slot_match, pair_slot[None, :], 0), axis=1)
    group_first = column_index[None, :] < (degrees - group_pair)[:, None]
    spectra_six = spectra.reshape(lat_count, 4, pair_local, 2, radii, colats)
    arrived = lax.all_to_all(spectra_six, "lat", split_axis=0, concat_axis=5, tiled=True)[0]
    raw_sums = jnp.einsum(
        "qsfrt,stk->qsfrk",
        arrived,
        lax.all_gather(analysis, "rad", axis=1, tiled=True),
        preferred_element_type=jnp.float32,
    )
    slot_first = column_index[None, :] < (degrees - pair_slot)[:, None]
    coefficient = jnp.where(slot_first[None, :, None, None, :], raw_sums[:2], raw_sums[2:]).astype(
        jnp.bfloat16
    )
    coefficient = coefficient.reshape(2, group_total, radii, coef_count)
    coefficient = lax.all_to_all(coefficient, "rad", split_axis=1, concat_axis=2, tiled=True)
    degree = jnp.where(
        group_first, group_pair[:, None] + column_index[None, :], column_index[None, :] - 1
    ).astype(jnp.float32)
    field_zero = group_field == 0
    right_group = jnp.where(field_zero[:, None, None], rad_right[0], rad_right[1])
    left_group = jnp.where(field_zero[:, None, None], rad_left[0], rad_left[1])
    rates_group = jnp.where(field_zero[:, None], rad_rates[0], rad_rates[1])
    damping = 1.0 / (
        rates_group[:, :, None]
        + 2.0 * degree[:, None, :] * (degree[:, None, :] + 1.0) / (degrees * degrees)
    )
    mixed_sum = jnp.einsum(
        "cgrk,gqr->cgqk", coefficient, right_group, preferred_element_type=jnp.float32
    )
    scaled = (mixed_sum * damping[None]).astype(jnp.bfloat16)
    solved = jnp.einsum(
        "cgqk,grq->grck", scaled, left_group, preferred_element_type=jnp.float32
    ).astype(jnp.bfloat16)
    returned = lax.all_to_all(solved, "rad", split_axis=1, concat_axis=0, tiled=True)
    return returned.reshape(pair_local, 2, radii, 2, coef_count)


def local(*args):
    entropy, analysis = args[0], args[5]
    radii, colats, longitudes = entropy.shape
    slots = analysis.shape[0]
    rads = lax.axis_size("rad")
    fits = 2 * radii == LANES and colats % STEP == 0 and longitudes % LANES == 0
    fits = fits and rads & (rads - 1) == 0 and analysis.shape[1] % 16 == 0
    columns = 4 * lax.axis_size("lat")
    if fits and slots % (8 * rads) == 0 and columns * rads % LANES == 0:
        unit = slots // 8
        return local_chunks([2 * unit, 3 * unit, 2 * unit, unit], *args)
    return local_plain(*args)


def solution(mesh):
    placed = (
        P("rad", "lat", None),
        P("rad", "lat", None),
        P("rad"),
        P("rad"),
        P("lat"),
        P("lat", "rad", None),
        P(),
        P(),
        P(),
    )
    return jax.shard_map(
        local,
        mesh=mesh,
        in_specs=placed,
        out_specs=P("lat", None, "rad", None, None),
        check_vma=False,
    )
```

```python
import functools
import math

import jax
import jax.numpy as jnp
from jax import lax
from jax.experimental import pallas as pl
from jax.experimental.pallas import tpu as pltpu
from jax.sharding import PartitionSpec as P

LANES = 128
STEP = 16
VMEM_BYTES = 56 * 1024 * 1024
COST = 1024
SIZES = (12, 8, 6, 4, 2)
ORDER = "L0 R0 P0 S2 L1 R1 P1 S3 L2 R2 P2 S4 L3 R3 L4 P3 R4 P4"


def fourier_kernel(parts, slope, gravity, entropy_ref, flow_ref, basis_ref, *refs):
    out_refs, (rows_s, product_s, out_s) = refs[: len(parts)], refs[len(parts) :]
    fields, radii, step, longitudes = rows_s.shape
    dests, width = out_refs[0].shape[0], out_refs[0].shape[3]
    columns = sum(parts)
    blocks = dests * columns // LANES

    def radius(r, carry):
        entropy_f = entropy_ref[r].astype(jnp.float32)
        flow_f = flow_ref[r].astype(jnp.float32)
        heating = -flow_f * (slope[r] + entropy_f)
        buoyant = gravity[r] * entropy_f - 0.5 * flow_f * flow_f
        rows_s[0, r] = heating.astype(jnp.bfloat16)
        rows_s[1, r] = buoyant.astype(jnp.bfloat16)
        return carry

    lax.fori_loop(0, radii, radius, 0)

    def field(f, carry):
        product = jnp.dot(
            rows_s[f].reshape(radii * step, longitudes),
            basis_ref[...],
            preferred_element_type=jnp.float32,
        )
        for b in range(blocks):
            start = pl.multiple_of(f * (radii * step), radii * step)
            product_s[b, pl.ds(start, radii * step), :] = product[:, b * LANES : (b + 1) * LANES]
        return carry

    lax.fori_loop(0, fields, field, 0)

    def turn(b, carry):
        for t in range(step):
            turned = product_s[b, pl.ds(t, width, stride=step), :].T
            out_s[pl.ds(b * (LANES * step) + t, LANES, stride=step), :] = turned
        return carry

    lax.fori_loop(0, blocks, turn, 0)
    whole = out_s[...].reshape(dests, columns, step, width).astype(jnp.bfloat16)
    first = 0
    for part, out_ref in zip(parts, out_refs):
        out_ref[...] = whole[:, first : first + part]
        first += part


def fourier(entropy, flow, slope, gravity, basis, dests, parts, begin, end):
    radii, _, longitudes = entropy.shape
    width, columns = 2 * radii, sum(parts)
    grid_in = pl.BlockSpec((radii, STEP, longitudes), lambda i, *_: (0, begin // STEP + i, 0))
    return pl.pallas_call(
        functools.partial(fourier_kernel, parts),
        grid_spec=pltpu.PrefetchScalarGridSpec(
            num_scalar_prefetch=2,
            grid=((end - begin) // STEP,),
            in_specs=[
                grid_in,
                grid_in,
                pl.BlockSpec(basis.shape, lambda i, *_: (0, 0), pipeline_mode=pl.Buffered(1)),
            ],
            out_specs=[
                pl.BlockSpec((dests, part, STEP, width), lambda i, *_: (0, 0, i, 0))
                for part in parts
            ],
            scratch_shapes=[
                pltpu.VMEM((2, radii, STEP, longitudes), jnp.bfloat16),
                pltpu.VMEM((dests * columns // LANES, width * STEP, LANES), jnp.float32),
                pltpu.VMEM((dests * columns * STEP, width), jnp.float32),
            ],
        ),
        out_shape=[
            jax.ShapeDtypeStruct((dests, part, end - begin, width), jnp.bfloat16)
            for part in parts
        ],
        compiler_params=pltpu.CompilerParams(vmem_limit_bytes=VMEM_BYTES),
        cost_estimate=pl.CostEstimate(flops=COST, bytes_accessed=COST, transcendentals=0),
        name="fourier",
    )(slope, gravity, entropy, flow, basis)


def legendre_kernel(rads, degrees, scalars, *refs):
    spectra_refs, table_ref, out_refs = refs[: -rads - 1], refs[-rads - 1], refs[-rads:]
    parts, _, part, count = table_ref.shape
    per_rad, _, radii, padded = out_refs[0].shape
    width = 2 * radii
    slot = pl.program_id(0)
    me = scalars[0]
    pair = scalars[1 + slot]

    def column(q):
        pieces = [ref[:, 0, q] for ref in spectra_refs]
        piece = pieces[0] if len(pieces) == 1 else jnp.concatenate(pieces, axis=1)
        return piece.reshape(parts * part, width)

    raw = lax.dot_general(
        jnp.concatenate([column(q) for q in range(4)], axis=1),
        table_ref[:, 0].reshape(parts * part, count),
        (((0,), (0,)), ((), ())),
        preferred_element_type=jnp.float32,
    )
    k = lax.broadcasted_iota(jnp.int32, (width, count), 1)
    first = k < degrees - pair
    values = [
        jnp.where(
            first, raw[c * width : (c + 1) * width], raw[(2 + c) * width : (3 + c) * width]
        ).astype(jnp.bfloat16)
        for c in range(2)
    ]
    for f in range(2):
        group = 2 * slot + f
        owner, index = lax.div(group, per_rad), lax.rem(group, per_rad)
        for m in range(rads):

            @pl.when(owner ^ me == m)
            def _():
                for c in range(2):
                    out_refs[m][index, c, :, count - 1 :] = jnp.zeros(
                        (radii, padded - count + 1), jnp.bfloat16
                    )
                    out_refs[m][index, c, :, :count] = values[c][f * radii : (f + 1) * radii]


def legendre(spectra, table, scalars, rads, base, degrees):
    slots, width = spectra[0].shape[1], spectra[0].shape[4]
    parts, _, part, count = table.shape
    shape = (2 * slots // rads, 2, width // 2, pl.cdiv(count, LANES) * LANES)
    return pl.pallas_call(
        functools.partial(legendre_kernel, rads, degrees),
        grid_spec=pltpu.PrefetchScalarGridSpec(
            num_scalar_prefetch=1,
            grid=(slots,),
            in_specs=[
                pl.BlockSpec(
                    (piece.shape[0], 1) + piece.shape[2:], lambda s, _: (0, s, 0, 0, 0)
                )
                for piece in spectra
            ]
            + [pl.BlockSpec((parts, 1, part, count), lambda s, _: (0, base + s, 0, 0))],
            out_specs=[pl.BlockSpec(shape, lambda s, _: (0, 0, 0, 0))] * rads,
        ),
        out_shape=[jax.ShapeDtypeStruct(shape, jnp.bfloat16)] * rads,
        compiler_params=pltpu.CompilerParams(vmem_limit_bytes=VMEM_BYTES),
        cost_estimate=pl.CostEstimate(flops=COST, bytes_accessed=COST, transcendentals=0),
        name="legendre",
    )(scalars, *spectra, table)


def radial_kernel(rads, degrees, scalars, *refs):
    in_refs, (right_ref, left_ref, rates_ref) = refs[:rads], refs[rads : rads + 3]
    out_refs = refs[rads + 3 : 2 * rads + 3]
    gathered, scaled = refs[2 * rads + 3 :]
    _, _, radii, count = in_refs[0].shape
    me = scalars[0]
    group = me * pl.num_programs(0) + pl.program_id(0)
    pair = scalars[1 + lax.div(group, 2)]
    total = rads * radii
    k = lax.broadcasted_iota(jnp.int32, (1, count), 1)
    degree = jnp.where(k < degrees - pair, pair + k, k - 1).astype(jnp.float32)
    decay = 2.0 * degree * (degree + 1.0) / (degrees * degrees)
    damping = 1.0 / (rates_ref[0] + decay)
    for m in range(rads):
        start = pl.multiple_of((me ^ m) * radii, radii)
        for c in range(2):
            gathered[c, pl.ds(start, radii), :] = in_refs[m][0, c]
    for c in range(2):
        mixed = jnp.dot(right_ref[0], gathered[c], preferred_element_type=jnp.float32)
        scaled[c * total : (c + 1) * total] = (mixed * damping).astype(jnp.bfloat16)
    for m in range(rads):
        start = pl.multiple_of((me ^ m) * 2 * radii, 2 * radii)
        out_refs[m][0] = jnp.dot(
            left_ref[0, pl.ds(start, 2 * radii), :], scaled[...], preferred_element_type=jnp.float32
        ).astype(jnp.bfloat16)


def radial(pieces, right, left, rates, scalars, degrees):
    rads = len(pieces)
    per_rad, parts, radii, count = pieces[0].shape
    total = rads * radii

    def by_field(shape):
        return pl.BlockSpec((1,) + shape, lambda i, s: (lax.rem(s[0] * per_rad + i, 2), 0, 0))

    return pl.pallas_call(
        functools.partial(radial_kernel, rads, degrees),
        grid_spec=pltpu.PrefetchScalarGridSpec(
            num_scalar_prefetch=1,
            grid=(per_rad,),
            in_specs=[pl.BlockSpec((1, parts, radii, count), lambda i, s: (i, 0, 0, 0))] * rads
            + [by_field((total, total)), by_field((2 * total, 2 * total)), by_field((total, 1))],
            out_specs=[pl.BlockSpec((1, 2 * radii, count), lambda i, s: (i, 0, 0))] * rads,
            scratch_shapes=[
                pltpu.VMEM((2, total, count), jnp.bfloat16),
                pltpu.VMEM((2 * total, count), jnp.bfloat16),
            ],
        ),
        out_shape=[jax.ShapeDtypeStruct((per_rad, 2 * radii, count), jnp.bfloat16)] * rads,
        compiler_params=pltpu.CompilerParams(vmem_limit_bytes=VMEM_BYTES),
        cost_estimate=pl.CostEstimate(flops=COST, bytes_accessed=COST, transcendentals=0),
        name="radial",
    )(scalars, *pieces, right, left, rates)


def place_kernel(rads, base, scalars, *refs):
    in_refs, (out_ref, held, sems) = refs[:rads], refs[-3:]
    _, per_rad, radii, _, count = held.shape
    copies = []
    for m in range(rads):

        def one(g, carry):
            rows = in_refs[m][g]
            held[m, g] = rows.reshape(radii, 2, rows.shape[1])[:, :, :count]
            return carry

        lax.fori_loop(0, per_rad, one, 0)
        first = base + (scalars[0] ^ m) * per_rad
        copies.append(
            pltpu.make_async_copy(held.at[m], out_ref.at[pl.ds(first, per_rad)], sems.at[m])
        )
        copies[-1].start()
    for copy in copies:
        copy.wait()


def place(pieces, scalars, so_far, groups, base, count):
    rads = len(pieces)
    per_rad, rows, padded = pieces[0].shape
    return pl.pallas_call(
        functools.partial(place_kernel, rads, base),
        grid_spec=pltpu.PrefetchScalarGridSpec(
            num_scalar_prefetch=1,
            grid=(1,),
            in_specs=[pl.BlockSpec(piece.shape, lambda i, s: (0, 0, 0)) for piece in pieces]
            + ([] if so_far is None else [pl.BlockSpec(memory_space=pl.ANY)]),
            out_specs=pl.BlockSpec(memory_space=pl.ANY),
            scratch_shapes=[
                pltpu.VMEM((rads, per_rad, rows // 2, 2, count), jnp.bfloat16),
                pltpu.SemaphoreType.DMA((rads,)),
            ],
        ),
        out_shape=jax.ShapeDtypeStruct((groups, rows // 2, 2, count), jnp.bfloat16),
        input_output_aliases={} if so_far is None else {1 + rads: 0},
        compiler_params=pltpu.CompilerParams(vmem_limit_bytes=VMEM_BYTES),
        cost_estimate=pl.CostEstimate(flops=COST, bytes_accessed=COST, transcendentals=0),
        name="place",
    )(scalars, *pieces, *([] if so_far is None else [so_far]))


def basis_of(pairs, degrees, longitudes):
    orders = jnp.stack([pairs, degrees - 1 - pairs], axis=2).reshape(-1)
    orders = jnp.repeat(orders, 2)[None, :].astype(jnp.float32)
    quarter = (jnp.arange(orders.shape[1], dtype=jnp.int32) % 2 * (longitudes // 4))[None, :]
    turns = jnp.arange(longitudes, dtype=jnp.int32)[:, None].astype(jnp.float32) * orders
    turns = turns + quarter.astype(jnp.float32)
    turns = turns - longitudes * jnp.round(turns * (1.0 / longitudes))
    angle = (longitudes // 4 - jnp.abs(turns)) * (2.0 * math.pi / longitudes)
    square = angle * angle
    series = 1.0 / math.factorial(13)
    for power in (11, 9, 7, 5, 3, 1):
        series = (-1.0) ** (power // 2) / math.factorial(power) + square * series
    return (series * angle * (1.0 / math.sqrt(longitudes))).astype(jnp.bfloat16)


def local_chunks(
    sizes,
    entropy, radial_flow, slope, gravity, pair_slot, analysis, rad_right, rad_left, rad_rates,
):
    lats = lax.axis_size("lat")
    rads = lax.axis_size("rad")
    radii, colats, longitudes = entropy.shape
    slots, _, count = analysis.shape
    degrees = count - 1
    width = 2 * radii
    starts = [sum(sizes[:j]) for j in range(len(sizes))]
    me = lax.axis_index("rad").astype(jnp.int32)
    every_pair = lax.all_gather(pair_slot, "lat", axis=0)
    table = lax.all_gather(analysis, "rad", axis=0)
    total = rads * radii
    rates = rad_rates[:, :, None]
    scalars = [
        jnp.concatenate([me[None], pair_slot[start : start + size]])
        for start, size in zip(starts, sizes)
    ]
    latest = []

    def after(value, *earlier):
        return lax.optimization_barrier((value,) + earlier)[0] if earlier else value

    def exchange(pieces):
        return [after(pieces[0], *latest)] + [
            lax.ppermute(piece, "rad", [(i, i ^ m) for i in range(rads)])
            for m, piece in enumerate(pieces)
            if m
        ]

    def basis_at(pairs, chunks):
        first, size = starts[chunks[0]], sum(sizes[j] for j in chunks)
        return basis_of(pairs[:, first : first + size], degrees, longitudes)

    def transform(basis, chunks, begin, end, *earlier):
        parts = [4 * sizes[j] for j in chunks]
        basis = after(basis, *latest, *earlier)
        spectra = fourier(
            entropy, radial_flow, slope, gravity, basis, lats, parts, begin, end
        )
        latest[:] = [spectra[0]]
        return spectra

    arrived = [[] for _ in sizes]

    def send(j, spectra):
        spectra = lax.all_to_all(after(spectra, *latest), "lat", 0, 0, tiled=True)
        arrived[j].append(spectra.reshape(lats, sizes[j], 4, spectra.shape[2], width))

    def coefs(j):
        spectra = [after(arrived[j][0], *latest)] + arrived[j][1:]
        pieces = legendre(spectra, table, scalars[j], rads, starts[j], degrees)
        latest[:] = [pieces[0]]
        return pieces

    def solve(j, pieces):
        pieces = radial(exchange(pieces), rad_right, spread, rates, scalars[j], degrees)
        latest[:] = [pieces[0]]
        return pieces

    def put(j, pieces, so_far):
        base = 2 * starts[j]
        result = place(exchange(pieces), scalars[j], so_far, 2 * slots, base, count)
        latest[:] = [result]
        return result

    cut = colats // STEP // 3 * STEP
    last = len(sizes) - 1
    basis = basis_at(every_pair, [0])
    spectra_a = transform(basis, [0], 0, cut)
    send(0, spectra_a[0])
    pairs_b, rad_left = after((every_pair, rad_left), *latest)
    spread = jnp.zeros((2, total, 2, 2, total), jnp.bfloat16)
    spread = spread.at[:, :, 0, 0].set(rad_left).at[:, :, 1, 1].set(rad_left)
    spread = spread.reshape(2, 2 * total, 2 * total)
    spectra_b = transform(basis, [0], cut, colats)
    send(0, spectra_b[0])
    rest = range(1, last + 1)
    basis = basis_at(after(pairs_b, *latest), rest)
    later = transform(basis, rest, 0, colats, arrived[0][0])
    send(1, later[0])
    pieces, result = [None] * len(sizes), None
    for step in ORDER.split():
        j = int(step[1:])
        if step[0] == "S":
            send(j, later[j - 1])
        elif step[0] == "L":
            pieces[j] = coefs(j)
        elif step[0] == "R":
            pieces[j] = solve(j, pieces[j])
        else:
            result = put(j, pieces[j], result)
    return result.reshape(slots, 2, radii, 2, count)


def local_plain(
    entropy, radial_flow, slope, gravity, pair_slot, analysis, rad_right, rad_left, rad_rates
):
    lat_count = lax.axis_size("lat")
    rad_count = lax.axis_size("rad")
    radii, colats, longitudes = entropy.shape
    pair_local = pair_slot.shape[0]
    coef_count = analysis.shape[2]
    degrees = coef_count - 1
    group_total = 2 * pair_local
    group_local = group_total // rad_count
    every_pair = lax.all_gather(pair_slot, "lat", axis=0, tiled=True)
    entropy_f = entropy.astype(jnp.float32)
    flow_f = radial_flow.astype(jnp.float32)
    heating = -flow_f * (slope[:, None, None] + entropy_f)
    buoyant = gravity[:, None, None] * entropy_f - 0.5 * flow_f * flow_f
    sources = jnp.stack([heating, buoyant]).astype(jnp.bfloat16)
    pair_grid = every_pair.reshape(lat_count, 1, pair_local)
    orders = jnp.concatenate([pair_grid, degrees - 1 - pair_grid], axis=1)
    phase_index = jnp.arange(longitudes, dtype=jnp.int32)
    turn_count = phase_index[:, None, None, None] * orders[None] % longitudes
    angles = turn_count.astype(jnp.float32) * (2.0 * math.pi / longitudes)
    scaling = 1.0 / math.sqrt(longitudes)
    basis_table = jnp.stack([jnp.cos(angles) * scaling, -jnp.sin(angles) * scaling], axis=3)
    basis_table = basis_table.reshape(longitudes, lat_count * 4 * pair_local).astype(jnp.bfloat16)
    spectra = jnp.einsum(
        "frtj,jc->cfrt", sources, basis_table, preferred_element_type=jnp.float32
    ).astype(jnp.bfloat16)
    column_index = jnp.arange(coef_count, dtype=jnp.int32)
    group_index = lax.axis_index("rad") * group_local + jnp.arange(group_local, dtype=jnp.int32)
    group_slot = group_index // 2
    group_field = group_index % 2
    slot_match = jnp.arange(pair_local, dtype=jnp.int32)[None, :] == group_slot[:, None]
    group_pair = jnp.sum(jnp.where(slot_match, pair_slot[None, :], 0), axis=1)
    group_first = column_index[None, :] < (degrees - group_pair)[:, None]
    spectra_six = spectra.reshape(lat_count, 4, pair_local, 2, radii, colats)
    arrived = lax.all_to_all(spectra_six, "lat", split_axis=0, concat_axis=5, tiled=True)[0]
    raw_sums = jnp.einsum(
        "qsfrt,stk->qsfrk",
        arrived,
        lax.all_gather(analysis, "rad", axis=1, tiled=True),
        preferred_element_type=jnp.float32,
    )
    slot_first = column_index[None, :] < (degrees - pair_slot)[:, None]
    coefficient = jnp.where(slot_first[None, :, None, None, :], raw_sums[:2], raw_sums[2:]).astype(
        jnp.bfloat16
    )
    coefficient = coefficient.reshape(2, group_total, radii, coef_count)
    coefficient = lax.all_to_all(coefficient, "rad", split_axis=1, concat_axis=2, tiled=True)
    degree = jnp.where(
        group_first, group_pair[:, None] + column_index[None, :], column_index[None, :] - 1
    ).astype(jnp.float32)
    field_zero = group_field == 0
    right_group = jnp.where(field_zero[:, None, None], rad_right[0], rad_right[1])
    left_group = jnp.where(field_zero[:, None, None], rad_left[0], rad_left[1])
    rates_group = jnp.where(field_zero[:, None], rad_rates[0], rad_rates[1])
    damping = 1.0 / (
        rates_group[:, :, None]
        + 2.0 * degree[:, None, :] * (degree[:, None, :] + 1.0) / (degrees * degrees)
    )
    mixed_sum = jnp.einsum(
        "cgrk,gqr->cgqk", coefficient, right_group, preferred_element_type=jnp.float32
    )
    scaled = (mixed_sum * damping[None]).astype(jnp.bfloat16)
    solved = jnp.einsum(
        "cgqk,grq->grck", scaled, left_group, preferred_element_type=jnp.float32
    ).astype(jnp.bfloat16)
    returned = lax.all_to_all(solved, "rad", split_axis=1, concat_axis=0, tiled=True)
    return returned.reshape(pair_local, 2, radii, 2, coef_count)


def local(*args):
    entropy, analysis = args[0], args[5]
    radii, colats, longitudes = entropy.shape
    slots = analysis.shape[0]
    rads = lax.axis_size("rad")
    fits = 2 * radii == LANES and colats % STEP == 0 and longitudes % LANES == 0
    fits = fits and rads & (rads - 1) == 0 and analysis.shape[1] % 16 == 0
    columns = 4 * lax.axis_size("lat")
    if fits and slots % (8 * rads) == 0 and columns * rads % LANES == 0:
        return local_chunks([size * slots // sum(SIZES) for size in SIZES], *args)
    return local_plain(*args)


def solution(mesh):
    placed = (
        P("rad", "lat", None),
        P("rad", "lat", None),
        P("rad"),
        P("rad"),
        P("lat"),
        P("lat", "rad", None),
        P(),
        P(),
        P(),
    )
    return jax.shard_map(
        local,
        mesh=mesh,
        in_specs=placed,
        out_specs=P("lat", None, "rad", None, None),
        check_vma=False,
    )
```

```python
import functools
import math

import jax
import jax.numpy as jnp
from jax import lax
from jax.experimental import pallas as pl
from jax.experimental.pallas import tpu as pltpu
from jax.sharding import PartitionSpec as P

LANES = 128
STEP = 16
GROUP = 16
VMEM_BYTES = 56 * 1024 * 1024
COST = 1024
SIZES = ((6, 6), (4, 4), (4, 2), (2, 2), (2,))
ORDER = (
    ("L0", "L1", "R0", "R1", "P0", "P1", "S2", "L2", "L3", "R2", "R3", "P2", "P3", "S3"),
    ("L4", "L5", "R4", "R5", "P4", "P5", "S4", "L6", "L7", "R6", "R7", "P6", "L8", "P7"),
    ("R8", "P8"),
)


def fourier_kernel(parts, slope, gravity, entropy_ref, flow_ref, basis_ref, *refs):
    out_refs, (even_s, odd_s, product_s, out_s) = refs[: len(parts)], refs[len(parts) :]
    fields, group, step, longitudes = even_s.shape
    dests, width = out_refs[0].shape[0], out_refs[0].shape[3]
    radii, columns = width // fields, sum(parts)
    groups, blocks = radii // group, dests * columns // LANES
    run = group * step

    def sources(g, rows_s):
        for i in range(group):
            r = g * group + i
            entropy_f = entropy_ref[r].astype(jnp.float32)
            flow_f = flow_ref[r].astype(jnp.float32)
            heating = -flow_f * (slope[r] + entropy_f)
            buoyant = gravity[r] * entropy_f - 0.5 * flow_f * flow_f
            rows_s[0, i] = heating.astype(jnp.bfloat16)
            rows_s[1, i] = buoyant.astype(jnp.bfloat16)

    def multiply(g, rows_s):
        product = jnp.dot(
            rows_s[...].reshape(fields * run, longitudes),
            basis_ref[...],
            preferred_element_type=jnp.float32,
        )
        for b in range(blocks):
            for f in range(fields):
                start = pl.multiple_of((f * groups + g) * run, run)
                product_s[b, pl.ds(start, run), :] = product[
                    f * run : (f + 1) * run, b * LANES : (b + 1) * LANES
                ]

    sources(0, even_s)

    def two(i, carry):
        multiply(2 * i, even_s)
        sources(2 * i + 1, odd_s)
        multiply(2 * i + 1, odd_s)
        sources(jnp.minimum(2 * i + 2, groups - 1), even_s)
        return carry

    lax.fori_loop(0, groups // 2, two, 0)

    def turn(b, carry):
        for t in range(step):
            turned = product_s[b, pl.ds(t, width, stride=step), :].T
            out_s[pl.ds(b * (LANES * step) + t, LANES, stride=step), :] = turned
        return carry

    lax.fori_loop(0, blocks, turn, 0)
    whole = out_s[...].reshape(dests, columns, step, width).astype(jnp.bfloat16)
    first = 0
    for part, out_ref in zip(parts, out_refs):
        out_ref[...] = whole[:, first : first + part]
        first += part


def fourier(entropy, flow, slope, gravity, basis, dests, parts, begin, end, step):
    radii, _, longitudes = entropy.shape
    width, columns = 2 * radii, sum(parts)
    grid_in = pl.BlockSpec((radii, step, longitudes), lambda i, *_: (0, begin // step + i, 0))
    return pl.pallas_call(
        functools.partial(fourier_kernel, parts),
        grid_spec=pltpu.PrefetchScalarGridSpec(
            num_scalar_prefetch=2,
            grid=((end - begin) // step,),
            in_specs=[
                grid_in,
                grid_in,
                pl.BlockSpec(basis.shape, lambda i, *_: (0, 0), pipeline_mode=pl.Buffered(1)),
            ],
            out_specs=[
                pl.BlockSpec((dests, part, step, width), lambda i, *_: (0, 0, i, 0))
                for part in parts
            ],
            scratch_shapes=[
                pltpu.VMEM((2, GROUP, step, longitudes), jnp.bfloat16),
                pltpu.VMEM((2, GROUP, step, longitudes), jnp.bfloat16),
                pltpu.VMEM((dests * columns // LANES, width * step, LANES), jnp.float32),
                pltpu.VMEM((dests * columns * step, width), jnp.float32),
            ],
        ),
        out_shape=[
            jax.ShapeDtypeStruct((dests, part, end - begin, width), jnp.bfloat16)
            for part in parts
        ],
        compiler_params=pltpu.CompilerParams(vmem_limit_bytes=VMEM_BYTES),
        cost_estimate=pl.CostEstimate(flops=COST, bytes_accessed=COST, transcendentals=0),
        name="fourier",
    )(slope, gravity, entropy, flow, basis)


def legendre_kernel(rads, degrees, scalars, *refs):
    spectra_refs, table_ref, out_refs = refs[: -rads - 1], refs[-rads - 1], refs[-rads:]
    parts, _, part, count = table_ref.shape
    per_rad, _, radii, padded = out_refs[0].shape
    width = 2 * radii
    slot = pl.program_id(0)
    me = scalars[0]
    pair = scalars[1 + slot]

    def column(q):
        pieces = [ref[:, 0, q] for ref in spectra_refs]
        piece = pieces[0] if len(pieces) == 1 else jnp.concatenate(pieces, axis=1)
        return piece.reshape(parts * part, width)

    raw = lax.dot_general(
        jnp.concatenate([column(q) for q in range(4)], axis=1),
        table_ref[:, 0].reshape(parts * part, count),
        (((0,), (0,)), ((), ())),
        preferred_element_type=jnp.float32,
    )
    k = lax.broadcasted_iota(jnp.int32, (width, count), 1)
    first = k < degrees - pair
    values = [
        jnp.where(
            first, raw[c * width : (c + 1) * width], raw[(2 + c) * width : (3 + c) * width]
        ).astype(jnp.bfloat16)
        for c in range(2)
    ]
    for f in range(2):
        group = 2 * slot + f
        owner, index = lax.div(group, per_rad), lax.rem(group, per_rad)
        for m in range(rads):

            @pl.when(owner ^ me == m)
            def _():
                for c in range(2):
                    out_refs[m][index, c, :, count - 1 :] = jnp.zeros(
                        (radii, padded - count + 1), jnp.bfloat16
                    )
                    out_refs[m][index, c, :, :count] = values[c][f * radii : (f + 1) * radii]


def legendre(spectra, table, scalars, rads, offset, base, degrees):
    slots, width = scalars.shape[0] - 1, spectra[0].shape[4]
    parts, _, part, count = table.shape
    shape = (2 * slots // rads, 2, width // 2, pl.cdiv(count, LANES) * LANES)
    return pl.pallas_call(
        functools.partial(legendre_kernel, rads, degrees),
        grid_spec=pltpu.PrefetchScalarGridSpec(
            num_scalar_prefetch=1,
            grid=(slots,),
            in_specs=[
                pl.BlockSpec(
                    (piece.shape[0], 1) + piece.shape[2:], lambda s, _: (0, offset + s, 0, 0, 0)
                )
                for piece in spectra
            ]
            + [pl.BlockSpec((parts, 1, part, count), lambda s, _: (0, base + s, 0, 0))],
            out_specs=[pl.BlockSpec(shape, lambda s, _: (0, 0, 0, 0))] * rads,
        ),
        out_shape=[jax.ShapeDtypeStruct(shape, jnp.bfloat16)] * rads,
        compiler_params=pltpu.CompilerParams(vmem_limit_bytes=VMEM_BYTES),
        cost_estimate=pl.CostEstimate(flops=COST, bytes_accessed=COST, transcendentals=0),
        name="legendre",
    )(scalars, *spectra, table)


def radial_kernel(rads, degrees, scalars, *refs):
    in_refs, (right_ref, left_ref, rates_ref) = refs[:rads], refs[rads : rads + 3]
    out_refs = refs[rads + 3 : 2 * rads + 3]
    gathered, scaled = refs[2 * rads + 3 :]
    _, _, radii, count = in_refs[0].shape
    me = scalars[0]
    group = me * pl.num_programs(0) + pl.program_id(0)
    pair = scalars[1 + lax.div(group, 2)]
    total = rads * radii
    k = lax.broadcasted_iota(jnp.int32, (1, count), 1)
    degree = jnp.where(k < degrees - pair, pair + k, k - 1).astype(jnp.float32)
    decay = 2.0 * degree * (degree + 1.0) / (degrees * degrees)
    damping = 1.0 / (rates_ref[0] + decay)
    for m in range(rads):
        start = pl.multiple_of((me ^ m) * radii, radii)
        for c in range(2):
            gathered[c, pl.ds(start, radii), :] = in_refs[m][0, c]
    for c in range(2):
        mixed = jnp.dot(right_ref[0], gathered[c], preferred_element_type=jnp.float32)
        scaled[c * total : (c + 1) * total] = (mixed * damping).astype(jnp.bfloat16)
    for m in range(rads):
        start = pl.multiple_of((me ^ m) * 2 * radii, 2 * radii)
        out_refs[m][0] = jnp.dot(
            left_ref[0, pl.ds(start, 2 * radii), :], scaled[...], preferred_element_type=jnp.float32
        ).astype(jnp.bfloat16)


def radial(pieces, right, left, rates, scalars, degrees):
    rads = len(pieces)
    per_rad, parts, radii, count = pieces[0].shape
    total = rads * radii

    def by_field(shape):
        return pl.BlockSpec((1,) + shape, lambda i, s: (lax.rem(s[0] * per_rad + i, 2), 0, 0))

    return pl.pallas_call(
        functools.partial(radial_kernel, rads, degrees),
        grid_spec=pltpu.PrefetchScalarGridSpec(
            num_scalar_prefetch=1,
            grid=(per_rad,),
            in_specs=[pl.BlockSpec((1, parts, radii, count), lambda i, s: (i, 0, 0, 0))] * rads
            + [by_field((total, total)), by_field((2 * total, 2 * total)), by_field((total, 1))],
            out_specs=[pl.BlockSpec((1, 2 * radii, count), lambda i, s: (i, 0, 0))] * rads,
            scratch_shapes=[
                pltpu.VMEM((2, total, count), jnp.bfloat16),
                pltpu.VMEM((2 * total, count), jnp.bfloat16),
            ],
        ),
        out_shape=[jax.ShapeDtypeStruct((per_rad, 2 * radii, count), jnp.bfloat16)] * rads,
        compiler_params=pltpu.CompilerParams(vmem_limit_bytes=VMEM_BYTES),
        cost_estimate=pl.CostEstimate(flops=COST, bytes_accessed=COST, transcendentals=0),
        name="radial",
    )(scalars, *pieces, right, left, rates)


def place_kernel(rads, base, scalars, *refs):
    in_refs, (out_ref, held, sems) = refs[:rads], refs[-3:]
    _, per_rad, radii, _, count = held.shape
    copies = []
    for m in range(rads):

        def one(g, carry):
            rows = in_refs[m][g]
            held[m, g] = rows.reshape(radii, 2, rows.shape[1])[:, :, :count]
            return carry

        lax.fori_loop(0, per_rad, one, 0)
        first = base + (scalars[0] ^ m) * per_rad
        copies.append(
            pltpu.make_async_copy(held.at[m], out_ref.at[pl.ds(first, per_rad)], sems.at[m])
        )
        copies[-1].start()
    for copy in copies:
        copy.wait()


def place(pieces, scalars, so_far, groups, base, count):
    rads = len(pieces)
    per_rad, rows, padded = pieces[0].shape
    return pl.pallas_call(
        functools.partial(place_kernel, rads, base),
        grid_spec=pltpu.PrefetchScalarGridSpec(
            num_scalar_prefetch=1,
            grid=(1,),
            in_specs=[pl.BlockSpec(piece.shape, lambda i, s: (0, 0, 0)) for piece in pieces]
            + ([] if so_far is None else [pl.BlockSpec(memory_space=pl.ANY)]),
            out_specs=pl.BlockSpec(memory_space=pl.ANY),
            scratch_shapes=[
                pltpu.VMEM((rads, per_rad, rows // 2, 2, count), jnp.bfloat16),
                pltpu.SemaphoreType.DMA((rads,)),
            ],
        ),
        out_shape=jax.ShapeDtypeStruct((groups, rows // 2, 2, count), jnp.bfloat16),
        input_output_aliases={} if so_far is None else {1 + rads: 0},
        compiler_params=pltpu.CompilerParams(vmem_limit_bytes=VMEM_BYTES),
        cost_estimate=pl.CostEstimate(flops=COST, bytes_accessed=COST, transcendentals=0),
        name="place",
    )(scalars, *pieces, *([] if so_far is None else [so_far]))


def basis_of(pairs, degrees, longitudes):
    orders = jnp.stack([pairs, degrees - 1 - pairs], axis=2).reshape(-1)
    orders = jnp.repeat(orders, 2)[None, :].astype(jnp.float32)
    quarter = (jnp.arange(orders.shape[1], dtype=jnp.int32) % 2 * (longitudes // 4))[None, :]
    turns = jnp.arange(longitudes, dtype=jnp.int32)[:, None].astype(jnp.float32) * orders
    turns = turns + quarter.astype(jnp.float32)
    turns = turns - longitudes * jnp.round(turns * (1.0 / longitudes))
    angle = (longitudes // 4 - jnp.abs(turns)) * (2.0 * math.pi / longitudes)
    square = angle * angle
    series = 1.0 / math.factorial(13)
    for power in (11, 9, 7, 5, 3, 1):
        series = (-1.0) ** (power // 2) / math.factorial(power) + square * series
    return (series * angle * (1.0 / math.sqrt(longitudes))).astype(jnp.bfloat16)


def local_chunks(
    parts,
    entropy, radial_flow, slope, gravity, pair_slot, analysis, rad_right, rad_left, rad_rates,
):
    lats = lax.axis_size("lat")
    rads = lax.axis_size("rad")
    radii, colats, longitudes = entropy.shape
    slots, _, count = analysis.shape
    degrees = count - 1
    width = 2 * radii
    sizes = [sum(part) for part in parts]
    starts = [sum(sizes[:j]) for j in range(len(sizes))]
    units = [
        (j, sum(part[:i]), part[i]) for j, part in enumerate(parts) for i in range(len(part))
    ]
    me = lax.axis_index("rad").astype(jnp.int32)
    every_pair = lax.all_gather(pair_slot, "lat", axis=0)
    table = lax.all_gather(analysis, "rad", axis=0)
    total = rads * radii
    rates = rad_rates[:, :, None]
    scalars = [
        jnp.concatenate([me[None], pair_slot[starts[j] + offset :][:size]])
        for j, offset, size in units
    ]
    latest = []

    def after(value, *earlier):
        return lax.optimization_barrier((value,) + earlier)[0] if earlier else value

    def exchange(pieces):
        return [after(pieces[0], *latest)] + [
            lax.ppermute(piece, "rad", [(i, i ^ m) for i in range(rads)])
            for m, piece in enumerate(pieces)
            if m
        ]

    def basis_at(pairs, chunks):
        first, size = starts[chunks[0]], sum(sizes[j] for j in chunks)
        return basis_of(pairs[:, first : first + size], degrees, longitudes)

    def transform(basis, chunks, begin, end, step, *earlier):
        parts = [4 * sizes[j] for j in chunks]
        basis = after(basis, *latest, *earlier)
        spectra = fourier(
            entropy, radial_flow, slope, gravity, basis, lats, parts, begin, end, step
        )
        latest[:] = [spectra[0]]
        return spectra

    arrived = [[] for _ in sizes]

    def send(j, spectra):
        spectra = lax.all_to_all(after(spectra, *latest), "lat", 0, 0, tiled=True)
        arrived[j].append(spectra.reshape(lats, sizes[j], 4, spectra.shape[2], width))

    def coefs(u):
        j, offset, _ = units[u]
        spectra = [after(arrived[j][0], *latest)] + arrived[j][1:]
        base = starts[j] + offset
        pieces = legendre(spectra, table, scalars[u], rads, offset, base, degrees)
        latest[:] = [pieces[0]]
        return pieces

    def solve(u, pieces):
        pieces = radial(exchange(pieces), rad_right, spread, rates, scalars[u], degrees)
        latest[:] = [pieces[0]]
        return pieces

    def put(u, pieces, so_far):
        base = 2 * (starts[units[u][0]] + units[u][1])
        result = place(exchange(pieces), scalars[u], so_far, 2 * slots, base, count)
        latest[:] = [result]
        return result

    cut = STEP
    last = len(sizes) - 1
    basis = basis_at(every_pair, [0])
    spectra_a = transform(basis, [0], 0, cut, STEP // 2)
    send(0, spectra_a[0])
    pairs_b, rad_left = after((every_pair, rad_left), *latest)
    spread = jnp.zeros((2, total, 2, 2, total), jnp.bfloat16)
    spread = spread.at[:, :, 0, 0].set(rad_left).at[:, :, 1, 1].set(rad_left)
    spread = spread.reshape(2, 2 * total, 2 * total)
    spectra_b = transform(basis, [0], cut, colats, STEP)
    send(0, spectra_b[0])
    rest = range(1, last + 1)
    basis = basis_at(after(pairs_b, *latest), rest)
    later = transform(basis, rest, 0, colats, STEP, arrived[0][0])
    send(1, later[0])
    pieces, result = [None] * len(units), None
    for step in sum(ORDER, ()):
        j = int(step[1:])
        if step[0] == "S":
            send(j, later[j - 1])
        elif step[0] == "L":
            pieces[j] = coefs(j)
        elif step[0] == "R":
            pieces[j] = solve(j, pieces[j])
        else:
            result = put(j, pieces[j], result)
    return result.reshape(slots, 2, radii, 2, count)


def local_plain(
    entropy, radial_flow, slope, gravity, pair_slot, analysis, rad_right, rad_left, rad_rates
):
    lat_count = lax.axis_size("lat")
    rad_count = lax.axis_size("rad")
    radii, colats, longitudes = entropy.shape
    pair_local = pair_slot.shape[0]
    coef_count = analysis.shape[2]
    degrees = coef_count - 1
    group_total = 2 * pair_local
    group_local = group_total // rad_count
    every_pair = lax.all_gather(pair_slot, "lat", axis=0, tiled=True)
    entropy_f = entropy.astype(jnp.float32)
    flow_f = radial_flow.astype(jnp.float32)
    heating = -flow_f * (slope[:, None, None] + entropy_f)
    buoyant = gravity[:, None, None] * entropy_f - 0.5 * flow_f * flow_f
    sources = jnp.stack([heating, buoyant]).astype(jnp.bfloat16)
    pair_grid = every_pair.reshape(lat_count, 1, pair_local)
    orders = jnp.concatenate([pair_grid, degrees - 1 - pair_grid], axis=1)
    phase_index = jnp.arange(longitudes, dtype=jnp.int32)
    turn_count = phase_index[:, None, None, None] * orders[None] % longitudes
    angles = turn_count.astype(jnp.float32) * (2.0 * math.pi / longitudes)
    scaling = 1.0 / math.sqrt(longitudes)
    basis_table = jnp.stack([jnp.cos(angles) * scaling, -jnp.sin(angles) * scaling], axis=3)
    basis_table = basis_table.reshape(longitudes, lat_count * 4 * pair_local).astype(jnp.bfloat16)
    spectra = jnp.einsum(
        "frtj,jc->cfrt", sources, basis_table, preferred_element_type=jnp.float32
    ).astype(jnp.bfloat16)
    column_index = jnp.arange(coef_count, dtype=jnp.int32)
    group_index = lax.axis_index("rad") * group_local + jnp.arange(group_local, dtype=jnp.int32)
    group_slot = group_index // 2
    group_field = group_index % 2
    slot_match = jnp.arange(pair_local, dtype=jnp.int32)[None, :] == group_slot[:, None]
    group_pair = jnp.sum(jnp.where(slot_match, pair_slot[None, :], 0), axis=1)
    group_first = column_index[None, :] < (degrees - group_pair)[:, None]
    spectra_six = spectra.reshape(lat_count, 4, pair_local, 2, radii, colats)
    arrived = lax.all_to_all(spectra_six, "lat", split_axis=0, concat_axis=5, tiled=True)[0]
    raw_sums = jnp.einsum(
        "qsfrt,stk->qsfrk",
        arrived,
        lax.all_gather(analysis, "rad", axis=1, tiled=True),
        preferred_element_type=jnp.float32,
    )
    slot_first = column_index[None, :] < (degrees - pair_slot)[:, None]
    coefficient = jnp.where(slot_first[None, :, None, None, :], raw_sums[:2], raw_sums[2:]).astype(
        jnp.bfloat16
    )
    coefficient = coefficient.reshape(2, group_total, radii, coef_count)
    coefficient = lax.all_to_all(coefficient, "rad", split_axis=1, concat_axis=2, tiled=True)
    degree = jnp.where(
        group_first, group_pair[:, None] + column_index[None, :], column_index[None, :] - 1
    ).astype(jnp.float32)
    field_zero = group_field == 0
    right_group = jnp.where(field_zero[:, None, None], rad_right[0], rad_right[1])
    left_group = jnp.where(field_zero[:, None, None], rad_left[0], rad_left[1])
    rates_group = jnp.where(field_zero[:, None], rad_rates[0], rad_rates[1])
    damping = 1.0 / (
        rates_group[:, :, None]
        + 2.0 * degree[:, None, :] * (degree[:, None, :] + 1.0) / (degrees * degrees)
    )
    mixed_sum = jnp.einsum(
        "cgrk,gqr->cgqk", coefficient, right_group, preferred_element_type=jnp.float32
    )
    scaled = (mixed_sum * damping[None]).astype(jnp.bfloat16)
    solved = jnp.einsum(
        "cgqk,grq->grck", scaled, left_group, preferred_element_type=jnp.float32
    ).astype(jnp.bfloat16)
    returned = lax.all_to_all(solved, "rad", split_axis=1, concat_axis=0, tiled=True)
    return returned.reshape(pair_local, 2, radii, 2, coef_count)


def local(*args):
    entropy, analysis = args[0], args[5]
    radii, colats, longitudes = entropy.shape
    slots = analysis.shape[0]
    rads = lax.axis_size("rad")
    fits = 2 * radii == LANES and colats % STEP == 0 and longitudes % LANES == 0
    fits = fits and radii % (2 * GROUP) == 0 and colats > STEP
    fits = fits and rads & (rads - 1) == 0 and analysis.shape[1] % 16 == 0
    columns = 4 * lax.axis_size("lat")
    if fits and slots % (8 * rads) == 0 and columns * rads % LANES == 0:
        unit = slots // sum(sum(part) for part in SIZES)
        return local_chunks([[unit * size for size in part] for part in SIZES], *args)
    return local_plain(*args)


def solution(mesh):
    placed = (
        P("rad", "lat", None),
        P("rad", "lat", None),
        P("rad"),
        P("rad"),
        P("lat"),
        P("lat", "rad", None),
        P(),
        P(),
        P(),
    )
    return jax.shard_map(
        local,
        mesh=mesh,
        in_specs=placed,
        out_specs=P("lat", None, "rad", None, None),
        check_vma=False,
    )
```

```python
import functools
import math

import jax
import jax.numpy as jnp
from jax import lax
from jax.experimental import pallas as pl
from jax.experimental.pallas import tpu as pltpu
from jax.sharding import PartitionSpec as P

LANES = 128
STEP = 16
GROUP = 8
VMEM_BYTES = 56 * 1024 * 1024
COST = 1024
SIZES = ((6, 6), (8,), (6,), (2, 2), (2,))
ORDER = (
    ("L0", "L1", "R0", "R1", "P0", "P1", "S2", "L2", "R2", "P2", "S3", "L3", "R3", "P3", "S4"),
    ("L4", "L5", "R4", "R5", "P4", "L6", "P5", "R6", "P6"),
)


def fourier_kernel(parts, slope, gravity, entropy_ref, flow_ref, basis_ref, *refs):
    out_refs, (even_s, odd_s, product_s, out_s) = refs[: len(parts)], refs[len(parts) :]
    fields, group, step, longitudes = even_s.shape
    dests, width = out_refs[0].shape[0], out_refs[0].shape[3]
    radii, columns = width // fields, sum(parts)
    groups, blocks = radii // group, dests * columns // LANES
    run = group * step

    def sources(g, rows_s):
        for i in range(group):
            r = g * group + i
            entropy_f = entropy_ref[r].astype(jnp.float32)
            flow_f = flow_ref[r].astype(jnp.float32)
            heating = -flow_f * (slope[r] + entropy_f)
            buoyant = gravity[r] * entropy_f - 0.5 * flow_f * flow_f
            rows_s[0, i] = heating.astype(jnp.bfloat16)
            rows_s[1, i] = buoyant.astype(jnp.bfloat16)

    def multiply(g, rows_s):
        product = jnp.dot(
            rows_s[...].reshape(fields * run, longitudes),
            basis_ref[...],
            preferred_element_type=jnp.float32,
        )
        for b in range(blocks):
            for f in range(fields):
                start = pl.multiple_of((f * groups + g) * run, run)
                product_s[b, pl.ds(start, run), :] = product[
                    f * run : (f + 1) * run, b * LANES : (b + 1) * LANES
                ]

    sources(0, even_s)

    def two(i, carry):
        multiply(2 * i, even_s)
        sources(2 * i + 1, odd_s)
        multiply(2 * i + 1, odd_s)
        sources(jnp.minimum(2 * i + 2, groups - 1), even_s)
        return carry

    lax.fori_loop(0, groups // 2, two, 0)

    def turn(b, carry):
        for t in range(step):
            turned = product_s[b, pl.ds(t, width, stride=step), :].T
            out_s[pl.ds(b * (LANES * step) + t, LANES, stride=step), :] = turned
        return carry

    lax.fori_loop(0, blocks, turn, 0)
    whole = out_s[...].reshape(dests, columns, step, width).astype(jnp.bfloat16)
    first = 0
    for part, out_ref in zip(parts, out_refs):
        out_ref[...] = whole[:, first : first + part]
        first += part


def fourier(entropy, flow, slope, gravity, basis, dests, parts, begin, end, step):
    radii, _, longitudes = entropy.shape
    width, columns = 2 * radii, sum(parts)
    grid_in = pl.BlockSpec((radii, step, longitudes), lambda i, *_: (0, begin // step + i, 0))
    return pl.pallas_call(
        functools.partial(fourier_kernel, parts),
        grid_spec=pltpu.PrefetchScalarGridSpec(
            num_scalar_prefetch=2,
            grid=((end - begin) // step,),
            in_specs=[
                grid_in,
                grid_in,
                pl.BlockSpec(basis.shape, lambda i, *_: (0, 0), pipeline_mode=pl.Buffered(1)),
            ],
            out_specs=[
                pl.BlockSpec((dests, part, step, width), lambda i, *_: (0, 0, i, 0))
                for part in parts
            ],
            scratch_shapes=[
                pltpu.VMEM((2, GROUP, step, longitudes), jnp.bfloat16),
                pltpu.VMEM((2, GROUP, step, longitudes), jnp.bfloat16),
                pltpu.VMEM((dests * columns // LANES, width * step, LANES), jnp.float32),
                pltpu.VMEM((dests * columns * step, width), jnp.float32),
            ],
        ),
        out_shape=[
            jax.ShapeDtypeStruct((dests, part, end - begin, width), jnp.bfloat16)
            for part in parts
        ],
        compiler_params=pltpu.CompilerParams(vmem_limit_bytes=VMEM_BYTES),
        cost_estimate=pl.CostEstimate(flops=COST, bytes_accessed=COST, transcendentals=0),
        name="fourier",
    )(slope, gravity, entropy, flow, basis)


def legendre_kernel(rads, degrees, scalars, *refs):
    spectra_refs, table_ref, out_refs = refs[: -rads - 1], refs[-rads - 1], refs[-rads:]
    parts, _, part, count = table_ref.shape
    per_rad, _, radii, padded = out_refs[0].shape
    width = 2 * radii
    slot = pl.program_id(0)
    me = scalars[0]
    pair = scalars[1 + slot]

    def column(q):
        pieces = [ref[:, 0, q] for ref in spectra_refs]
        piece = pieces[0] if len(pieces) == 1 else jnp.concatenate(pieces, axis=1)
        return piece.reshape(parts * part, width)

    raw = lax.dot_general(
        jnp.concatenate([column(q) for q in range(4)], axis=1),
        table_ref[:, 0].reshape(parts * part, count),
        (((0,), (0,)), ((), ())),
        preferred_element_type=jnp.float32,
    )
    k = lax.broadcasted_iota(jnp.int32, (width, count), 1)
    first = k < degrees - pair
    values = [
        jnp.where(
            first, raw[c * width : (c + 1) * width], raw[(2 + c) * width : (3 + c) * width]
        ).astype(jnp.bfloat16)
        for c in range(2)
    ]
    for f in range(2):
        group = 2 * slot + f
        owner, index = lax.div(group, per_rad), lax.rem(group, per_rad)
        for m in range(rads):

            @pl.when(owner ^ me == m)
            def _():
                for c in range(2):
                    out_refs[m][index, c, :, count - 1 :] = jnp.zeros(
                        (radii, padded - count + 1), jnp.bfloat16
                    )
                    out_refs[m][index, c, :, :count] = values[c][f * radii : (f + 1) * radii]


def legendre(spectra, table, scalars, rads, offset, base, degrees):
    slots, width = scalars.shape[0] - 1, spectra[0].shape[4]
    parts, _, part, count = table.shape
    shape = (2 * slots // rads, 2, width // 2, pl.cdiv(count, LANES) * LANES)
    return pl.pallas_call(
        functools.partial(legendre_kernel, rads, degrees),
        grid_spec=pltpu.PrefetchScalarGridSpec(
            num_scalar_prefetch=1,
            grid=(slots,),
            in_specs=[
                pl.BlockSpec(
                    (piece.shape[0], 1) + piece.shape[2:], lambda s, _: (0, offset + s, 0, 0, 0)
                )
                for piece in spectra
            ]
            + [pl.BlockSpec((parts, 1, part, count), lambda s, _: (0, base + s, 0, 0))],
            out_specs=[pl.BlockSpec(shape, lambda s, _: (0, 0, 0, 0))] * rads,
        ),
        out_shape=[jax.ShapeDtypeStruct(shape, jnp.bfloat16)] * rads,
        compiler_params=pltpu.CompilerParams(vmem_limit_bytes=VMEM_BYTES),
        cost_estimate=pl.CostEstimate(flops=COST, bytes_accessed=COST, transcendentals=0),
        name="legendre",
    )(scalars, *spectra, table)


def radial_kernel(rads, degrees, scalars, *refs):
    in_refs, (right_ref, left_ref, rates_ref) = refs[:rads], refs[rads : rads + 3]
    out_refs = refs[rads + 3 : 2 * rads + 3]
    gathered, scaled = refs[2 * rads + 3 :]
    _, _, radii, count = in_refs[0].shape
    me = scalars[0]
    group = me * pl.num_programs(0) + pl.program_id(0)
    pair = scalars[1 + lax.div(group, 2)]
    total = rads * radii
    k = lax.broadcasted_iota(jnp.int32, (1, count), 1)
    degree = jnp.where(k < degrees - pair, pair + k, k - 1).astype(jnp.float32)
    decay = 2.0 * degree * (degree + 1.0) / (degrees * degrees)
    damping = 1.0 / (rates_ref[0] + decay)
    for m in range(rads):
        start = pl.multiple_of((me ^ m) * radii, radii)
        for c in range(2):
            gathered[c, pl.ds(start, radii), :] = in_refs[m][0, c]
    for c in range(2):
        mixed = jnp.dot(right_ref[0], gathered[c], preferred_element_type=jnp.float32)
        scaled[c * total : (c + 1) * total] = (mixed * damping).astype(jnp.bfloat16)
    for m in range(rads):
        start = pl.multiple_of((me ^ m) * 2 * radii, 2 * radii)
        out_refs[m][0] = jnp.dot(
            left_ref[0, pl.ds(start, 2 * radii), :], scaled[...], preferred_element_type=jnp.float32
        ).astype(jnp.bfloat16)


def radial(pieces, right, left, rates, scalars, degrees):
    rads = len(pieces)
    per_rad, parts, radii, count = pieces[0].shape
    total = rads * radii

    def by_field(shape):
        return pl.BlockSpec((1,) + shape, lambda i, s: (lax.rem(s[0] * per_rad + i, 2), 0, 0))

    return pl.pallas_call(
        functools.partial(radial_kernel, rads, degrees),
        grid_spec=pltpu.PrefetchScalarGridSpec(
            num_scalar_prefetch=1,
            grid=(per_rad,),
            in_specs=[pl.BlockSpec((1, parts, radii, count), lambda i, s: (i, 0, 0, 0))] * rads
            + [by_field((total, total)), by_field((2 * total, 2 * total)), by_field((total, 1))],
            out_specs=[pl.BlockSpec((1, 2 * radii, count), lambda i, s: (i, 0, 0))] * rads,
            scratch_shapes=[
                pltpu.VMEM((2, total, count), jnp.bfloat16),
                pltpu.VMEM((2 * total, count), jnp.bfloat16),
            ],
        ),
        out_shape=[jax.ShapeDtypeStruct((per_rad, 2 * radii, count), jnp.bfloat16)] * rads,
        compiler_params=pltpu.CompilerParams(vmem_limit_bytes=VMEM_BYTES),
        cost_estimate=pl.CostEstimate(flops=COST, bytes_accessed=COST, transcendentals=0),
        name="radial",
    )(scalars, *pieces, right, left, rates)


def place_kernel(rads, base, scalars, *refs):
    in_refs, (out_ref, taken, held, in_sems, out_sems) = refs[:rads], refs[-5:]
    _, per_rad, rows, padded = taken.shape
    count = held.shape[4]
    reads = [
        pltpu.make_async_copy(in_refs[m], taken.at[m], in_sems.at[m]) for m in range(rads)
    ]
    for copy in reads:
        copy.start()
    for copy in reads:
        copy.wait()

    def one(g, carry):
        m, index = lax.div(g, per_rad), lax.rem(g, per_rad)
        held[m, index] = taken[m, index].reshape(rows // 2, 2, padded)[:, :, :count]
        return carry

    lax.fori_loop(0, rads * per_rad, one, 0)
    writes = [
        pltpu.make_async_copy(
            held.at[m],
            out_ref.at[pl.ds(base + (scalars[0] ^ m) * per_rad, per_rad)],
            out_sems.at[m],
        )
        for m in range(rads)
    ]
    for copy in writes:
        copy.start()
    for copy in writes:
        copy.wait()


def place(pieces, scalars, so_far, groups, base, count):
    rads = len(pieces)
    per_rad, rows, padded = pieces[0].shape
    return pl.pallas_call(
        functools.partial(place_kernel, rads, base),
        grid_spec=pltpu.PrefetchScalarGridSpec(
            num_scalar_prefetch=1,
            grid=(1,),
            in_specs=[pl.BlockSpec(memory_space=pl.ANY)]
            * (rads if so_far is None else rads + 1),
            out_specs=pl.BlockSpec(memory_space=pl.ANY),
            scratch_shapes=[
                pltpu.VMEM((rads, per_rad, rows, padded), jnp.bfloat16),
                pltpu.VMEM((rads, per_rad, rows // 2, 2, count), jnp.bfloat16),
                pltpu.SemaphoreType.DMA((rads,)),
                pltpu.SemaphoreType.DMA((rads,)),
            ],
        ),
        out_shape=jax.ShapeDtypeStruct((groups, rows // 2, 2, count), jnp.bfloat16),
        input_output_aliases={} if so_far is None else {1 + rads: 0},
        compiler_params=pltpu.CompilerParams(vmem_limit_bytes=VMEM_BYTES),
        cost_estimate=pl.CostEstimate(flops=COST, bytes_accessed=COST, transcendentals=0),
        name="place",
    )(scalars, *pieces, *([] if so_far is None else [so_far]))


def basis_of(pairs, degrees, longitudes):
    orders = jnp.stack([pairs, degrees - 1 - pairs], axis=2).reshape(-1)
    orders = jnp.repeat(orders, 2)[None, :].astype(jnp.float32)
    quarter = (jnp.arange(orders.shape[1], dtype=jnp.int32) % 2 * (longitudes // 4))[None, :]
    turns = jnp.arange(longitudes, dtype=jnp.int32)[:, None].astype(jnp.float32) * orders
    turns = turns + quarter.astype(jnp.float32)
    turns = turns - longitudes * jnp.round(turns * (1.0 / longitudes))
    angle = (longitudes // 4 - jnp.abs(turns)) * (2.0 * math.pi / longitudes)
    square = angle * angle
    series = 1.0 / math.factorial(13)
    for power in (11, 9, 7, 5, 3, 1):
        series = (-1.0) ** (power // 2) / math.factorial(power) + square * series
    return (series * angle * (1.0 / math.sqrt(longitudes))).astype(jnp.bfloat16)


def local_chunks(
    parts,
    entropy, radial_flow, slope, gravity, pair_slot, analysis, rad_right, rad_left, rad_rates,
):
    lats = lax.axis_size("lat")
    rads = lax.axis_size("rad")
    radii, colats, longitudes = entropy.shape
    slots, _, count = analysis.shape
    degrees = count - 1
    width = 2 * radii
    sizes = [sum(part) for part in parts]
    starts = [sum(sizes[:j]) for j in range(len(sizes))]
    units = [
        (j, sum(part[:i]), part[i]) for j, part in enumerate(parts) for i in range(len(part))
    ]
    me = lax.axis_index("rad").astype(jnp.int32)
    every_pair = lax.all_gather(pair_slot, "lat", axis=0)
    table = lax.all_gather(analysis, "rad", axis=0)
    total = rads * radii
    rates = rad_rates[:, :, None]
    scalars = [
        jnp.concatenate([me[None], pair_slot[starts[j] + offset :][:size]])
        for j, offset, size in units
    ]
    latest = []

    def after(value, *earlier):
        return lax.optimization_barrier((value,) + earlier)[0] if earlier else value

    def exchange(pieces):
        return [after(pieces[0], *latest)] + [
            lax.ppermute(piece, "rad", [(i, i ^ m) for i in range(rads)])
            for m, piece in enumerate(pieces)
            if m
        ]

    def basis_at(pairs, chunks):
        first, size = starts[chunks[0]], sum(sizes[j] for j in chunks)
        return basis_of(pairs[:, first : first + size], degrees, longitudes)

    def transform(basis, chunks, begin, end, step, *earlier):
        parts = [4 * sizes[j] for j in chunks]
        basis = after(basis, *latest, *earlier)
        spectra = fourier(
            entropy, radial_flow, slope, gravity, basis, lats, parts, begin, end, step
        )
        latest[:] = [spectra[0]]
        return spectra

    arrived = [[] for _ in sizes]

    def send(j, spectra):
        spectra = lax.all_to_all(after(spectra, *latest), "lat", 0, 0, tiled=True)
        arrived[j].append(spectra.reshape(lats, sizes[j], 4, spectra.shape[2], width))

    def coefs(u):
        j, offset, _ = units[u]
        spectra = [after(arrived[j][0], *latest)] + arrived[j][1:]
        base = starts[j] + offset
        pieces = legendre(spectra, table, scalars[u], rads, offset, base, degrees)
        latest[:] = [pieces[0]]
        return pieces

    def solve(u, pieces):
        pieces = radial(exchange(pieces), rad_right, spread, rates, scalars[u], degrees)
        latest[:] = [pieces[0]]
        return pieces

    def put(u, pieces, so_far):
        base = 2 * (starts[units[u][0]] + units[u][1])
        result = place(exchange(pieces), scalars[u], so_far, 2 * slots, base, count)
        latest[:] = [result]
        return result

    cut = STEP
    last = len(sizes) - 1
    basis = basis_at(every_pair, [0])
    spectra_a = transform(basis, [0], 0, cut, STEP // 2)
    send(0, spectra_a[0])
    pairs_b, rad_left = after((every_pair, rad_left), *latest)
    spread = jnp.zeros((2, total, 2, 2, total), jnp.bfloat16)
    spread = spread.at[:, :, 0, 0].set(rad_left).at[:, :, 1, 1].set(rad_left)
    spread = spread.reshape(2, 2 * total, 2 * total)
    spectra_b = transform(basis, [0], cut, colats, STEP)
    send(0, spectra_b[0])
    rest = range(1, last + 1)
    basis = basis_at(after(pairs_b, *latest), rest)
    later = transform(basis, rest, 0, colats, STEP, arrived[0][0])
    send(1, later[0])
    pieces, result = [None] * len(units), None
    for step in sum(ORDER, ()):
        j = int(step[1:])
        if step[0] == "S":
            send(j, later[j - 1])
        elif step[0] == "L":
            pieces[j] = coefs(j)
        elif step[0] == "R":
            pieces[j] = solve(j, pieces[j])
        else:
            result = put(j, pieces[j], result)
    return result.reshape(slots, 2, radii, 2, count)


def local_plain(
    entropy, radial_flow, slope, gravity, pair_slot, analysis, rad_right, rad_left, rad_rates
):
    lat_count = lax.axis_size("lat")
    rad_count = lax.axis_size("rad")
    radii, colats, longitudes = entropy.shape
    pair_local = pair_slot.shape[0]
    coef_count = analysis.shape[2]
    degrees = coef_count - 1
    group_total = 2 * pair_local
    group_local = group_total // rad_count
    every_pair = lax.all_gather(pair_slot, "lat", axis=0, tiled=True)
    entropy_f = entropy.astype(jnp.float32)
    flow_f = radial_flow.astype(jnp.float32)
    heating = -flow_f * (slope[:, None, None] + entropy_f)
    buoyant = gravity[:, None, None] * entropy_f - 0.5 * flow_f * flow_f
    sources = jnp.stack([heating, buoyant]).astype(jnp.bfloat16)
    pair_grid = every_pair.reshape(lat_count, 1, pair_local)
    orders = jnp.concatenate([pair_grid, degrees - 1 - pair_grid], axis=1)
    phase_index = jnp.arange(longitudes, dtype=jnp.int32)
    turn_count = phase_index[:, None, None, None] * orders[None] % longitudes
    angles = turn_count.astype(jnp.float32) * (2.0 * math.pi / longitudes)
    scaling = 1.0 / math.sqrt(longitudes)
    basis_table = jnp.stack([jnp.cos(angles) * scaling, -jnp.sin(angles) * scaling], axis=3)
    basis_table = basis_table.reshape(longitudes, lat_count * 4 * pair_local).astype(jnp.bfloat16)
    spectra = jnp.einsum(
        "frtj,jc->cfrt", sources, basis_table, preferred_element_type=jnp.float32
    ).astype(jnp.bfloat16)
    column_index = jnp.arange(coef_count, dtype=jnp.int32)
    group_index = lax.axis_index("rad") * group_local + jnp.arange(group_local, dtype=jnp.int32)
    group_slot = group_index // 2
    group_field = group_index % 2
    slot_match = jnp.arange(pair_local, dtype=jnp.int32)[None, :] == group_slot[:, None]
    group_pair = jnp.sum(jnp.where(slot_match, pair_slot[None, :], 0), axis=1)
    group_first = column_index[None, :] < (degrees - group_pair)[:, None]
    spectra_six = spectra.reshape(lat_count, 4, pair_local, 2, radii, colats)
    arrived = lax.all_to_all(spectra_six, "lat", split_axis=0, concat_axis=5, tiled=True)[0]
    raw_sums = jnp.einsum(
        "qsfrt,stk->qsfrk",
        arrived,
        lax.all_gather(analysis, "rad", axis=1, tiled=True),
        preferred_element_type=jnp.float32,
    )
    slot_first = column_index[None, :] < (degrees - pair_slot)[:, None]
    coefficient = jnp.where(slot_first[None, :, None, None, :], raw_sums[:2], raw_sums[2:]).astype(
        jnp.bfloat16
    )
    coefficient = coefficient.reshape(2, group_total, radii, coef_count)
    coefficient = lax.all_to_all(coefficient, "rad", split_axis=1, concat_axis=2, tiled=True)
    degree = jnp.where(
        group_first, group_pair[:, None] + column_index[None, :], column_index[None, :] - 1
    ).astype(jnp.float32)
    field_zero = group_field == 0
    right_group = jnp.where(field_zero[:, None, None], rad_right[0], rad_right[1])
    left_group = jnp.where(field_zero[:, None, None], rad_left[0], rad_left[1])
    rates_group = jnp.where(field_zero[:, None], rad_rates[0], rad_rates[1])
    damping = 1.0 / (
        rates_group[:, :, None]
        + 2.0 * degree[:, None, :] * (degree[:, None, :] + 1.0) / (degrees * degrees)
    )
    mixed_sum = jnp.einsum(
        "cgrk,gqr->cgqk", coefficient, right_group, preferred_element_type=jnp.float32
    )
    scaled = (mixed_sum * damping[None]).astype(jnp.bfloat16)
    solved = jnp.einsum(
        "cgqk,grq->grck", scaled, left_group, preferred_element_type=jnp.float32
    ).astype(jnp.bfloat16)
    returned = lax.all_to_all(solved, "rad", split_axis=1, concat_axis=0, tiled=True)
    return returned.reshape(pair_local, 2, radii, 2, coef_count)


def local(*args):
    entropy, analysis = args[0], args[5]
    radii, colats, longitudes = entropy.shape
    slots = analysis.shape[0]
    rads = lax.axis_size("rad")
    fits = 2 * radii == LANES and colats % STEP == 0 and longitudes % LANES == 0
    fits = fits and radii % (2 * GROUP) == 0 and colats > STEP
    fits = fits and rads & (rads - 1) == 0 and analysis.shape[1] % 16 == 0
    columns = 4 * lax.axis_size("lat")
    if fits and slots % (8 * rads) == 0 and columns * rads % LANES == 0:
        unit = slots // sum(sum(part) for part in SIZES)
        return local_chunks([[unit * size for size in part] for part in SIZES], *args)
    return local_plain(*args)


def solution(mesh):
    placed = (
        P("rad", "lat", None),
        P("rad", "lat", None),
        P("rad"),
        P("rad"),
        P("lat"),
        P("lat", "rad", None),
        P(),
        P(),
        P(),
    )
    return jax.shard_map(
        local,
        mesh=mesh,
        in_specs=placed,
        out_specs=P("lat", None, "rad", None, None),
        check_vma=False,
    )
```

```python
import functools
import math

import jax
import jax.numpy as jnp
from jax import lax
from jax.experimental import pallas as pl
from jax.experimental.pallas import tpu as pltpu
from jax.sharding import PartitionSpec as P

LANES = 128
STEP = 16
GROUP = 8
VMEM_BYTES = 56 * 1024 * 1024
COST = 1024
SIZES = ((6, 6), (8,), (6,), (2, 2), (2,))
ORDER = (
    ("L0", "L1", "R0", "R1", "P0", "P1", "S2", "L2", "R2", "P2", "S3", "L3", "R3", "P3", "S4"),
    ("L4", "L5", "R4", "R5", "P4", "L6", "P5", "R6", "P6"),
)


def fourier_kernel(parts, slope, gravity, entropy_ref, flow_ref, basis_ref, *refs):
    out_refs, (even_s, odd_s, product_s, out_s) = refs[: len(parts)], refs[len(parts) :]
    fields, group, step, longitudes = even_s.shape
    dests, width = out_refs[0].shape[0], out_refs[0].shape[3]
    radii, columns = width // fields, sum(parts)
    groups, blocks = radii // group, dests * columns // LANES
    run = group * step

    def sources(g, rows_s):
        for i in range(group):
            r = g * group + i
            entropy_f = entropy_ref[r].astype(jnp.float32)
            flow_f = flow_ref[r].astype(jnp.float32)
            heating = -flow_f * (slope[r] + entropy_f)
            buoyant = gravity[r] * entropy_f - 0.5 * flow_f * flow_f
            rows_s[0, i] = heating.astype(jnp.bfloat16)
            rows_s[1, i] = buoyant.astype(jnp.bfloat16)

    def multiply(g, rows_s):
        product = jnp.dot(
            rows_s[...].reshape(fields * run, longitudes),
            basis_ref[...],
            preferred_element_type=jnp.float32,
        )
        for b in range(blocks):
            for f in range(fields):
                start = pl.multiple_of((f * groups + g) * run, run)
                product_s[b, pl.ds(start, run), :] = product[
                    f * run : (f + 1) * run, b * LANES : (b + 1) * LANES
                ]

    sources(0, even_s)

    def two(i, carry):
        multiply(2 * i, even_s)
        sources(2 * i + 1, odd_s)
        multiply(2 * i + 1, odd_s)
        sources(jnp.minimum(2 * i + 2, groups - 1), even_s)
        return carry

    lax.fori_loop(0, groups // 2, two, 0)

    def turn(b, carry):
        for t in range(step):
            turned = product_s[b, pl.ds(t, width, stride=step), :].T
            out_s[pl.ds(b * (LANES * step) + t, LANES, stride=step), :] = turned
        return carry

    lax.fori_loop(0, blocks, turn, 0)
    whole = out_s[...].reshape(dests, columns, step, width).astype(jnp.bfloat16)
    first = 0
    for part, out_ref in zip(parts, out_refs):
        out_ref[...] = whole[:, first : first + part]
        first += part


def fourier(entropy, flow, slope, gravity, basis, dests, parts, begin, end, step):
    radii, _, longitudes = entropy.shape
    width, columns = 2 * radii, sum(parts)
    group = GROUP * STEP // step
    grid_in = pl.BlockSpec((radii, step, longitudes), lambda i, *_: (0, begin // step + i, 0))
    return pl.pallas_call(
        functools.partial(fourier_kernel, parts),
        grid_spec=pltpu.PrefetchScalarGridSpec(
            num_scalar_prefetch=2,
            grid=((end - begin) // step,),
            in_specs=[
                grid_in,
                grid_in,
                pl.BlockSpec(basis.shape, lambda i, *_: (0, 0), pipeline_mode=pl.Buffered(1)),
            ],
            out_specs=[
                pl.BlockSpec((dests, part, step, width), lambda i, *_: (0, 0, i, 0))
                for part in parts
            ],
            scratch_shapes=[
                pltpu.VMEM((2, group, step, longitudes), jnp.bfloat16),
                pltpu.VMEM((2, group, step, longitudes), jnp.bfloat16),
                pltpu.VMEM((dests * columns // LANES, width * step, LANES), jnp.float32),
                pltpu.VMEM((dests * columns * step, width), jnp.float32),
            ],
        ),
        out_shape=[
            jax.ShapeDtypeStruct((dests, part, end - begin, width), jnp.bfloat16)
            for part in parts
        ],
        compiler_params=pltpu.CompilerParams(vmem_limit_bytes=VMEM_BYTES),
        cost_estimate=pl.CostEstimate(flops=COST, bytes_accessed=COST, transcendentals=0),
        name="fourier",
    )(slope, gravity, entropy, flow, basis)


def legendre_kernel(rads, degrees, scalars, *refs):
    spectra_refs, table_ref, out_refs = refs[: -rads - 1], refs[-rads - 1], refs[-rads:]
    parts, _, part, count = table_ref.shape
    per_rad, _, radii, padded = out_refs[0].shape
    width = 2 * radii
    slot = pl.program_id(0)
    me = scalars[0]
    pair = scalars[1 + slot]

    def column(q):
        pieces = [ref[:, 0, q] for ref in spectra_refs]
        piece = pieces[0] if len(pieces) == 1 else jnp.concatenate(pieces, axis=1)
        return piece.reshape(parts * part, width)

    raw = lax.dot_general(
        jnp.concatenate([column(q) for q in range(4)], axis=1),
        table_ref[:, 0].reshape(parts * part, count),
        (((0,), (0,)), ((), ())),
        preferred_element_type=jnp.float32,
    )
    k = lax.broadcasted_iota(jnp.int32, (width, count), 1)
    first = k < degrees - pair
    values = [
        jnp.where(
            first, raw[c * width : (c + 1) * width], raw[(2 + c) * width : (3 + c) * width]
        ).astype(jnp.bfloat16)
        for c in range(2)
    ]
    for f in range(2):
        group = 2 * slot + f
        owner, index = lax.div(group, per_rad), lax.rem(group, per_rad)
        for m in range(rads):

            @pl.when(owner ^ me == m)
            def _():
                for c in range(2):
                    out_refs[m][index, c, :, count - 1 :] = jnp.zeros(
                        (radii, padded - count + 1), jnp.bfloat16
                    )
                    out_refs[m][index, c, :, :count] = values[c][f * radii : (f + 1) * radii]


def legendre(spectra, table, scalars, rads, offset, base, degrees):
    slots, width = scalars.shape[0] - 1, spectra[0].shape[4]
    parts, _, part, count = table.shape
    shape = (2 * slots // rads, 2, width // 2, pl.cdiv(count, LANES) * LANES)
    return pl.pallas_call(
        functools.partial(legendre_kernel, rads, degrees),
        grid_spec=pltpu.PrefetchScalarGridSpec(
            num_scalar_prefetch=1,
            grid=(slots,),
            in_specs=[
                pl.BlockSpec(
                    (piece.shape[0], 1) + piece.shape[2:], lambda s, _: (0, offset + s, 0, 0, 0)
                )
                for piece in spectra
            ]
            + [pl.BlockSpec((parts, 1, part, count), lambda s, _: (0, base + s, 0, 0))],
            out_specs=[pl.BlockSpec(shape, lambda s, _: (0, 0, 0, 0))] * rads,
        ),
        out_shape=[jax.ShapeDtypeStruct(shape, jnp.bfloat16)] * rads,
        compiler_params=pltpu.CompilerParams(vmem_limit_bytes=VMEM_BYTES),
        cost_estimate=pl.CostEstimate(flops=COST, bytes_accessed=COST, transcendentals=0),
        name="legendre",
    )(scalars, *spectra, table)


def radial_kernel(rads, degrees, scalars, *refs):
    in_refs, (right_ref, left_ref, rates_ref) = refs[:rads], refs[rads : rads + 3]
    out_refs = refs[rads + 3 : 2 * rads + 3]
    gathered, scaled = refs[2 * rads + 3 :]
    _, _, radii, count = in_refs[0].shape
    me = scalars[0]
    group = me * pl.num_programs(0) + pl.program_id(0)
    pair = scalars[1 + lax.div(group, 2)]
    total = rads * radii
    k = lax.broadcasted_iota(jnp.int32, (1, count), 1)
    degree = jnp.where(k < degrees - pair, pair + k, k - 1).astype(jnp.float32)
    decay = 2.0 * degree * (degree + 1.0) / (degrees * degrees)
    damping = 1.0 / (rates_ref[0] + decay)
    for m in range(rads):
        start = pl.multiple_of((me ^ m) * radii, radii)
        for c in range(2):
            gathered[c, pl.ds(start, radii), :] = in_refs[m][0, c]
    for c in range(2):
        mixed = jnp.dot(right_ref[0], gathered[c], preferred_element_type=jnp.float32)
        scaled[c * total : (c + 1) * total] = (mixed * damping).astype(jnp.bfloat16)
    for m in range(rads):
        start = pl.multiple_of((me ^ m) * 2 * radii, 2 * radii)
        out_refs[m][0] = jnp.dot(
            left_ref[0, pl.ds(start, 2 * radii), :], scaled[...], preferred_element_type=jnp.float32
        ).astype(jnp.bfloat16)


def radial(pieces, right, left, rates, scalars, degrees):
    rads = len(pieces)
    per_rad, parts, radii, count = pieces[0].shape
    total = rads * radii

    def by_field(shape):
        return pl.BlockSpec((1,) + shape, lambda i, s: (lax.rem(s[0] * per_rad + i, 2), 0, 0))

    return pl.pallas_call(
        functools.partial(radial_kernel, rads, degrees),
        grid_spec=pltpu.PrefetchScalarGridSpec(
            num_scalar_prefetch=1,
            grid=(per_rad,),
            in_specs=[pl.BlockSpec((1, parts, radii, count), lambda i, s: (i, 0, 0, 0))] * rads
            + [by_field((total, total)), by_field((2 * total, 2 * total)), by_field((total, 1))],
            out_specs=[pl.BlockSpec((1, 2 * radii, count), lambda i, s: (i, 0, 0))] * rads,
            scratch_shapes=[
                pltpu.VMEM((2, total, count), jnp.bfloat16),
                pltpu.VMEM((2 * total, count), jnp.bfloat16),
            ],
        ),
        out_shape=[jax.ShapeDtypeStruct((per_rad, 2 * radii, count), jnp.bfloat16)] * rads,
        compiler_params=pltpu.CompilerParams(vmem_limit_bytes=VMEM_BYTES),
        cost_estimate=pl.CostEstimate(flops=COST, bytes_accessed=COST, transcendentals=0),
        name="radial",
    )(scalars, *pieces, right, left, rates)


def place_kernel(rads, base, scalars, *refs):
    in_refs, (out_ref, taken, held, in_sems, out_sems) = refs[:rads], refs[-5:]
    _, per_rad, rows, padded = taken.shape
    count = held.shape[4]
    reads = [
        pltpu.make_async_copy(in_refs[m], taken.at[m], in_sems.at[m]) for m in range(rads)
    ]
    for copy in reads:
        copy.start()
    for copy in reads:
        copy.wait()

    def one(g, carry):
        m, index = lax.div(g, per_rad), lax.rem(g, per_rad)
        held[m, index] = taken[m, index].reshape(rows // 2, 2, padded)[:, :, :count]
        return carry

    lax.fori_loop(0, rads * per_rad, one, 0)
    writes = [
        pltpu.make_async_copy(
            held.at[m],
            out_ref.at[pl.ds(base + (scalars[0] ^ m) * per_rad, per_rad)],
            out_sems.at[m],
        )
        for m in range(rads)
    ]
    for copy in writes:
        copy.start()
    for copy in writes:
        copy.wait()


def place(pieces, scalars, so_far, groups, base, count):
    rads = len(pieces)
    per_rad, rows, padded = pieces[0].shape
    return pl.pallas_call(
        functools.partial(place_kernel, rads, base),
        grid_spec=pltpu.PrefetchScalarGridSpec(
            num_scalar_prefetch=1,
            grid=(1,),
            in_specs=[pl.BlockSpec(memory_space=pl.ANY)]
            * (rads if so_far is None else rads + 1),
            out_specs=pl.BlockSpec(memory_space=pl.ANY),
            scratch_shapes=[
                pltpu.VMEM((rads, per_rad, rows, padded), jnp.bfloat16),
                pltpu.VMEM((rads, per_rad, rows // 2, 2, count), jnp.bfloat16),
                pltpu.SemaphoreType.DMA((rads,)),
                pltpu.SemaphoreType.DMA((rads,)),
            ],
        ),
        out_shape=jax.ShapeDtypeStruct((groups, rows // 2, 2, count), jnp.bfloat16),
        input_output_aliases={} if so_far is None else {1 + rads: 0},
        compiler_params=pltpu.CompilerParams(vmem_limit_bytes=VMEM_BYTES),
        cost_estimate=pl.CostEstimate(flops=COST, bytes_accessed=COST, transcendentals=0),
        name="place",
    )(scalars, *pieces, *([] if so_far is None else [so_far]))


def basis_of(pairs, degrees, longitudes):
    orders = jnp.stack([pairs, degrees - 1 - pairs], axis=2).reshape(-1)
    orders = jnp.repeat(orders, 2)[None, :].astype(jnp.float32)
    quarter = (jnp.arange(orders.shape[1], dtype=jnp.int32) % 2 * (longitudes // 4))[None, :]
    turns = jnp.arange(longitudes, dtype=jnp.int32)[:, None].astype(jnp.float32) * orders
    turns = turns + quarter.astype(jnp.float32)
    turns = turns - longitudes * jnp.round(turns * (1.0 / longitudes))
    angle = (longitudes // 4 - jnp.abs(turns)) * (2.0 * math.pi / longitudes)
    square = angle * angle
    series = 1.0 / math.factorial(13)
    for power in (11, 9, 7, 5, 3, 1):
        series = (-1.0) ** (power // 2) / math.factorial(power) + square * series
    return (series * angle * (1.0 / math.sqrt(longitudes))).astype(jnp.bfloat16)


def local_chunks(
    parts,
    entropy, radial_flow, slope, gravity, pair_slot, analysis, rad_right, rad_left, rad_rates,
):
    lats = lax.axis_size("lat")
    rads = lax.axis_size("rad")
    radii, colats, longitudes = entropy.shape
    slots, _, count = analysis.shape
    degrees = count - 1
    width = 2 * radii
    sizes = [sum(part) for part in parts]
    starts = [sum(sizes[:j]) for j in range(len(sizes))]
    units = [
        (j, sum(part[:i]), part[i]) for j, part in enumerate(parts) for i in range(len(part))
    ]
    me = lax.axis_index("rad").astype(jnp.int32)
    every_pair = lax.all_gather(pair_slot, "lat", axis=0)
    table = lax.all_gather(analysis, "rad", axis=0)
    total = rads * radii
    rates = rad_rates[:, :, None]
    scalars = [
        jnp.concatenate([me[None], pair_slot[starts[j] + offset :][:size]])
        for j, offset, size in units
    ]
    latest = []

    def after(value, *earlier):
        return lax.optimization_barrier((value,) + earlier)[0] if earlier else value

    def exchange(pieces):
        return [after(pieces[0], *latest)] + [
            lax.ppermute(piece, "rad", [(i, i ^ m) for i in range(rads)])
            for m, piece in enumerate(pieces)
            if m
        ]

    def basis_at(pairs, chunks):
        first, size = starts[chunks[0]], sum(sizes[j] for j in chunks)
        return basis_of(pairs[:, first : first + size], degrees, longitudes)

    def transform(basis, chunks, begin, end, step, *earlier):
        parts = [4 * sizes[j] for j in chunks]
        basis = after(basis, *latest, *earlier)
        spectra = fourier(
            entropy, radial_flow, slope, gravity, basis, lats, parts, begin, end, step
        )
        latest[:] = [spectra[0]]
        return spectra

    arrived = [[] for _ in sizes]

    def send(j, spectra):
        spectra = lax.all_to_all(after(spectra, *latest), "lat", 0, 0, tiled=True)
        arrived[j].append(spectra.reshape(lats, sizes[j], 4, spectra.shape[2], width))

    def coefs(u):
        j, offset, _ = units[u]
        spectra = [after(arrived[j][0], *latest)] + arrived[j][1:]
        base = starts[j] + offset
        pieces = legendre(spectra, table, scalars[u], rads, offset, base, degrees)
        latest[:] = [pieces[0]]
        return pieces

    def solve(u, pieces):
        pieces = radial(exchange(pieces), rad_right, spread, rates, scalars[u], degrees)
        latest[:] = [pieces[0]]
        return pieces

    def put(u, pieces, so_far):
        base = 2 * (starts[units[u][0]] + units[u][1])
        result = place(exchange(pieces), scalars[u], so_far, 2 * slots, base, count)
        latest[:] = [result]
        return result

    cut = STEP
    last = len(sizes) - 1
    basis = basis_at(every_pair, [0])
    spectra_a = transform(basis, [0], 0, cut, STEP // 2)
    send(0, spectra_a[0])
    pairs_b, rad_left = after((every_pair, rad_left), *latest)
    spread = jnp.zeros((2, total, 2, 2, total), jnp.bfloat16)
    spread = spread.at[:, :, 0, 0].set(rad_left).at[:, :, 1, 1].set(rad_left)
    spread = spread.reshape(2, 2 * total, 2 * total)
    spectra_b = transform(basis, [0], cut, colats, STEP)
    send(0, spectra_b[0])
    rest = range(1, last + 1)
    basis = basis_at(after(pairs_b, *latest), rest)
    later = transform(basis, rest, 0, colats, STEP, arrived[0][0])
    send(1, later[0])
    pieces, result = [None] * len(units), None
    for step in sum(ORDER, ()):
        j = int(step[1:])
        if step[0] == "S":
            send(j, later[j - 1])
        elif step[0] == "L":
            pieces[j] = coefs(j)
        elif step[0] == "R":
            pieces[j] = solve(j, pieces[j])
        else:
            result = put(j, pieces[j], result)
    return result.reshape(slots, 2, radii, 2, count)


def local_plain(
    entropy, radial_flow, slope, gravity, pair_slot, analysis, rad_right, rad_left, rad_rates
):
    lat_count = lax.axis_size("lat")
    rad_count = lax.axis_size("rad")
    radii, colats, longitudes = entropy.shape
    pair_local = pair_slot.shape[0]
    coef_count = analysis.shape[2]
    degrees = coef_count - 1
    group_total = 2 * pair_local
    group_local = group_total // rad_count
    every_pair = lax.all_gather(pair_slot, "lat", axis=0, tiled=True)
    entropy_f = entropy.astype(jnp.float32)
    flow_f = radial_flow.astype(jnp.float32)
    heating = -flow_f * (slope[:, None, None] + entropy_f)
    buoyant = gravity[:, None, None] * entropy_f - 0.5 * flow_f * flow_f
    sources = jnp.stack([heating, buoyant]).astype(jnp.bfloat16)
    pair_grid = every_pair.reshape(lat_count, 1, pair_local)
    orders = jnp.concatenate([pair_grid, degrees - 1 - pair_grid], axis=1)
    phase_index = jnp.arange(longitudes, dtype=jnp.int32)
    turn_count = phase_index[:, None, None, None] * orders[None] % longitudes
    angles = turn_count.astype(jnp.float32) * (2.0 * math.pi / longitudes)
    scaling = 1.0 / math.sqrt(longitudes)
    basis_table = jnp.stack([jnp.cos(angles) * scaling, -jnp.sin(angles) * scaling], axis=3)
    basis_table = basis_table.reshape(longitudes, lat_count * 4 * pair_local).astype(jnp.bfloat16)
    spectra = jnp.einsum(
        "frtj,jc->cfrt", sources, basis_table, preferred_element_type=jnp.float32
    ).astype(jnp.bfloat16)
    column_index = jnp.arange(coef_count, dtype=jnp.int32)
    group_index = lax.axis_index("rad") * group_local + jnp.arange(group_local, dtype=jnp.int32)
    group_slot = group_index // 2
    group_field = group_index % 2
    slot_match = jnp.arange(pair_local, dtype=jnp.int32)[None, :] == group_slot[:, None]
    group_pair = jnp.sum(jnp.where(slot_match, pair_slot[None, :], 0), axis=1)
    group_first = column_index[None, :] < (degrees - group_pair)[:, None]
    spectra_six = spectra.reshape(lat_count, 4, pair_local, 2, radii, colats)
    arrived = lax.all_to_all(spectra_six, "lat", split_axis=0, concat_axis=5, tiled=True)[0]
    raw_sums = jnp.einsum(
        "qsfrt,stk->qsfrk",
        arrived,
        lax.all_gather(analysis, "rad", axis=1, tiled=True),
        preferred_element_type=jnp.float32,
    )
    slot_first = column_index[None, :] < (degrees - pair_slot)[:, None]
    coefficient = jnp.where(slot_first[None, :, None, None, :], raw_sums[:2], raw_sums[2:]).astype(
        jnp.bfloat16
    )
    coefficient = coefficient.reshape(2, group_total, radii, coef_count)
    coefficient = lax.all_to_all(coefficient, "rad", split_axis=1, concat_axis=2, tiled=True)
    degree = jnp.where(
        group_first, group_pair[:, None] + column_index[None, :], column_index[None, :] - 1
    ).astype(jnp.float32)
    field_zero = group_field == 0
    right_group = jnp.where(field_zero[:, None, None], rad_right[0], rad_right[1])
    left_group = jnp.where(field_zero[:, None, None], rad_left[0], rad_left[1])
    rates_group = jnp.where(field_zero[:, None], rad_rates[0], rad_rates[1])
    damping = 1.0 / (
        rates_group[:, :, None]
        + 2.0 * degree[:, None, :] * (degree[:, None, :] + 1.0) / (degrees * degrees)
    )
    mixed_sum = jnp.einsum(
        "cgrk,gqr->cgqk", coefficient, right_group, preferred_element_type=jnp.float32
    )
    scaled = (mixed_sum * damping[None]).astype(jnp.bfloat16)
    solved = jnp.einsum(
        "cgqk,grq->grck", scaled, left_group, preferred_element_type=jnp.float32
    ).astype(jnp.bfloat16)
    returned = lax.all_to_all(solved, "rad", split_axis=1, concat_axis=0, tiled=True)
    return returned.reshape(pair_local, 2, radii, 2, coef_count)


def local(*args):
    entropy, analysis = args[0], args[5]
    radii, colats, longitudes = entropy.shape
    slots = analysis.shape[0]
    rads = lax.axis_size("rad")
    fits = 2 * radii == LANES and colats % STEP == 0 and longitudes % LANES == 0
    fits = fits and radii % (4 * GROUP) == 0 and colats > STEP
    fits = fits and rads & (rads - 1) == 0 and analysis.shape[1] % 16 == 0
    columns = 4 * lax.axis_size("lat")
    if fits and slots % (8 * rads) == 0 and columns * rads % LANES == 0:
        unit = slots // sum(sum(part) for part in SIZES)
        return local_chunks([[unit * size for size in part] for part in SIZES], *args)
    return local_plain(*args)


def solution(mesh):
    placed = (
        P("rad", "lat", None),
        P("rad", "lat", None),
        P("rad"),
        P("rad"),
        P("lat"),
        P("lat", "rad", None),
        P(),
        P(),
        P(),
    )
    return jax.shard_map(
        local,
        mesh=mesh,
        in_specs=placed,
        out_specs=P("lat", None, "rad", None, None),
        check_vma=False,
    )
```
